128 devices in a mesh: tm: 4 (over y_lo, core), space: 32 (over x, y_hi, z).
Axes of the slice: x: 4, y: 4 (y_hi: 2, y_lo: 2; y = y_hi * 2 + y_lo), z: 4, core: 2. Of those that a mesh axis runs over, the one named last changes fastest.
Arguments:
- queries: bfloat16 [4, 32, 384, 1536], P('tm', 'space'), may hold values from -7 to 7
- keys: bfloat16 [4, 32, 384, 1536], P('tm', 'space'), may hold values from -7 to 7
- values: bfloat16 [4, 32, 384, 1536], P('tm', 'space'), may hold values from -2 to 2
- outputs: bfloat16 [4, 32, 384, 1536], P('tm', 'space'), may hold values from -2 to 2
- out_grads: bfloat16 [4, 32, 384, 1536], P('tm', 'space'), may hold values from -6 to 6
- log_sums: float32 [4, 32, 12, 384], P('tm', 'space'), may hold values from 8 to 9.5
- window_mask: int32 [4, 32, 9], P('tm', 'space'), may hold values 0 or 1
Outputs:
- query_grads: bfloat16 [4, 32, 384, 1536], P('tm', 'space')
- key_grads: bfloat16 [4, 32, 384, 1536], P('tm', 'space')
- value_grads: bfloat16 [4, 32, 384, 1536], P('tm', 'space')
The draws below stay inside these ranges and needn't reach their ends.
All inputs are finite; a program needn't handle non-finite values. No bound on the sum of `window_mask` on one device may be relied on, other than what follows from the above.
Results may differ from the reference program's by a relative error of at most 0.0065.
Values may be sent and summed in bfloat16 or wider, within the bound.
A program may use at most 192 MiB of HBM per device.

```python
import jax
import jax.numpy as jnp
from jax import lax

HEADS = 12
HEAD_DIM = 128
TILE = 384
WINDOW = 3
NT = 4
NR = 32


def place_ends(drawn, key, low, top_value):
    extent = drawn.shape
    place = [jax.random.randint(jax.random.fold_in(key, axis), (), 0, extent[axis]) for axis in range(len(extent))]
    drawn = drawn.at[tuple(place)].set(low)
    longest = extent.index(max(extent))
    place[longest] = (place[longest] + 1) % extent[longest]
    return drawn.at[tuple(place)].set(top_value)


def level_of(own_key, extent, cuts, smallest, high):
    factor_of, own = 1.0, jax.random.fold_in(own_key, 6)
    for position, blocks in cuts:
        steps = jnp.exp(jax.random.uniform(jax.random.fold_in(own, position), (blocks,), jnp.float32, smallest / len(cuts), high / len(cuts)))
        factor_of = factor_of * jnp.repeat(steps, extent[position] // blocks).reshape([-1 if axis == position else 1 for axis in range(len(extent))])
    return factor_of


def bell_draw(rng, extent, width, limit, shards=(), kind=jnp.bfloat16):
    entries = width * jax.random.normal(rng, extent, jnp.float32)
    if shards:
        entries = entries * level_of(rng, extent, shards, -0.22, 0.18)
    return jnp.clip(entries, -limit, limit).astype(kind)


def setup_inputs(seed: int = 0) -> dict:
    arg_keys = jax.random.split(jax.random.key(seed), 8)
    return {
        "queries": bell_draw(arg_keys[0], (NT, NR, TILE, HEADS * HEAD_DIM), 1.2, 7.0, ((0, 4), (1, 32))),
        "keys": bell_draw(arg_keys[1], (NT, NR, TILE, HEADS * HEAD_DIM), 1.2, 7.0, ((0, 4), (1, 32))),
        "values": bell_draw(arg_keys[2], (NT, NR, TILE, HEADS * HEAD_DIM), 0.3, 2.0, ((0, 4), (1, 32))),
        "outputs": bell_draw(arg_keys[3], (NT, NR, TILE, HEADS * HEAD_DIM), 0.3, 2.0, ((0, 4), (1, 32))),
        "out_grads": bell_draw(arg_keys[4], (NT, NR, TILE, HEADS * HEAD_DIM), 1.0, 6.0, ((0, 4), (1, 32))),
        "log_sums": jnp.clip(8.0 + 1.5 * jax.random.uniform(arg_keys[5], (NT, NR, HEADS, TILE), jnp.float32) ** level_of(arg_keys[5], (NT, NR, HEADS, TILE), ((0, 4), (1, 32)), -0.2, 0.2), 8.0, 9.5),
        "window_mask": place_ends((jax.random.randint(arg_keys[6], (NT, NR, WINDOW * WINDOW), 0, 4) < 3).astype(jnp.int32), jax.random.fold_in(arg_keys[6], 1), 0, 1),
    }


def round_keep(value):
    return lax.optimization_barrier(value.astype(jnp.bfloat16)).astype(jnp.float32)


def pair_terms(query_rows, grad_rows, sum_rows, delta_rows, flags, key_rows, value_rows):
    num_tiles = query_rows.shape[0]
    shape_four = (num_tiles, TILE, HEADS, HEAD_DIM)
    factor = HEAD_DIM ** -0.5
    query_heads = query_rows.reshape(shape_four).astype(jnp.float32)
    grad_heads = grad_rows.reshape(shape_four).astype(jnp.float32)
    key_heads = key_rows.reshape(shape_four).astype(jnp.float32)
    value_heads = value_rows.reshape(shape_four).astype(jnp.float32)
    scores = jnp.einsum("nqhd,nkhd->nhqk", query_heads, key_heads) * factor
    weights = jnp.exp(scores - sum_rows[..., None]) * flags[:, None, None, None]
    weights_low = round_keep(weights)
    grad_prob = jnp.einsum("nqhd,nkhd->nhqk", grad_heads, value_heads)
    grad_score = round_keep(weights * (grad_prob - delta_rows[..., None]))
    query_term = jnp.einsum("nhqk,nkhd->nqhd", grad_score, key_heads) * factor
    key_term = jnp.einsum("nhqk,nqhd->nkhd", grad_score, query_heads) * factor
    value_term = jnp.einsum("nhqk,nqhd->nkhd", weights_low, grad_heads)
    flat = (num_tiles, TILE, HEADS * HEAD_DIM)
    return query_term.reshape(flat), key_term.reshape(flat), value_term.reshape(flat)


def reference(queries, keys, values, outputs, out_grads, log_sums, window_mask):
    full_width = HEADS * HEAD_DIM
    padding = ((1, 1), (1, 1), (0, 0), (0, 0))
    keys_pad = jnp.pad(keys, padding)
    values_pad = jnp.pad(values, padding)
    products = out_grads.astype(jnp.float32) * outputs.astype(jnp.float32)
    deltas = products.reshape(NT, NR, TILE, HEADS, HEAD_DIM).sum(-1).transpose(0, 1, 3, 2)
    row_ids = jnp.arange(NR)

    def per_time(time_id):
        query_rows = lax.dynamic_index_in_dim(queries, time_id, 0, False)
        grad_rows = lax.dynamic_index_in_dim(out_grads, time_id, 0, False)
        sum_rows = lax.dynamic_index_in_dim(log_sums, time_id, 0, False)
        delta_rows = lax.dynamic_index_in_dim(deltas, time_id, 0, False)
        mask_rows = lax.dynamic_index_in_dim(window_mask, time_id, 0, False)
        query_total = jnp.zeros((NR, TILE, full_width), jnp.float32)
        grouped = []
        for time_off in (-1, 0, 1):
            inner = jnp.zeros((2, NR + 2, TILE, full_width), jnp.float32)
            key_plane = lax.dynamic_index_in_dim(keys_pad, time_id + 1 + time_off, 0, False)
            value_plane = lax.dynamic_index_in_dim(values_pad, time_id + 1 + time_off, 0, False)
            time_inside = jnp.logical_and(time_id + time_off >= 0, time_id + time_off < NT)
            for row_off in (-1, 0, 1):
                slot_index = (time_off + 1) * 3 + row_off + 1
                row_inside = jnp.logical_and(row_ids + row_off >= 0, row_ids + row_off < NR)
                if slot_index == 4:
                    picked = jnp.ones((NR,), jnp.float32)
                else:
                    picked = (mask_rows[:, slot_index] > 0).astype(jnp.float32)
                flags = picked * jnp.logical_and(row_inside, time_inside).astype(jnp.float32)
                key_rows = key_plane[1 + row_off:1 + row_off + NR]
                value_rows = value_plane[1 + row_off:1 + row_off + NR]
                query_term, key_term, value_term = pair_terms(query_rows, grad_rows, sum_rows, delta_rows, flags, key_rows, value_rows)
                query_total = query_total + query_term
                parts = round_keep(jnp.stack((key_term, value_term)))
                inner = inner.at[:, 1 + row_off:1 + row_off + NR].add(parts)
            grouped.append(inner[:, 1:NR + 1].astype(jnp.bfloat16))
        return query_total.astype(jnp.bfloat16), jnp.stack(grouped)

    query_grads, groups = lax.map(per_time, jnp.arange(NT))
    total = jnp.zeros((2, NT + 2, NR, TILE, full_width), jnp.float32)
    for time_off in (-1, 0, 1):
        piece = groups[:, time_off + 1].transpose(1, 0, 2, 3, 4).astype(jnp.float32)
        total = total.at[:, 1 + time_off:1 + time_off + NT].add(piece)
    key_grads = total[0, 1:NT + 1].astype(jnp.bfloat16)
    value_grads = total[1, 1:NT + 1].astype(jnp.bfloat16)
    return query_grads, key_grads, value_grads
```

```python
import functools
import math

import jax
import jax.numpy as jnp
from jax import lax
from jax.experimental import pallas as pl
from jax.experimental.pallas import tpu as pltpu
from jax.sharding import PartitionSpec as P

F32 = jnp.float32
LOW = jnp.bfloat16
MESH = pl.DeviceIdType.MESH
GROUP = 1
EARLY = 2
LOG2E = math.log2(math.e)
NT = (((1,), (1,)), ((), ()))
NN = (((1,), (0,)), ((), ()))
TN = (((0,), (0,)), ((), ()))
OWN, UP, DOWN = 0, 1, 2
CHIP, LINK = 1, 2
DELTA_ROW, PEN_ROW, AUX_ROWS = 16, 32, 48


def dot(a, b, dims):
    return lax.dot_general(a, b, dims, preferred_element_type=F32)


def kernel(
    q_in, k_in, v_in, o_in, g_in, lse_ref, mask_ref,
    dq_out, dk_out, dv_out,
    qs, gs, ks, vs, outs, aux, dq_acc, dq_own, dk_own, dv_own,
    dq_send, dk_send, dv_send, dq_recv, dk_recv, dv_recv,
    in_sem, q_ss, q_rs, kv_ss, kv_rs, aux_ss, aux_rs, dq_ss, dq_rs, dkv_ss, dkv_rs,
):
    tile, full = q_in.shape
    heads = lse_ref.shape[0]
    width = full // heads
    wide = GROUP * width
    chunks = heads // GROUP
    scale = width**-0.5
    frame, row = lax.axis_index("tm"), lax.axis_index("space")
    frames, rows = lax.axis_size("tm"), lax.axis_size("space")
    odd = lax.rem(frame, 2)
    step = 1 - 2 * odd
    has_up, has_down = row < rows - 1, row > 0
    other = frame - step
    has_link = jnp.logical_and(other >= 0, other < frames)
    to_up, to_down = (frame, row + 1), (frame, row - 1)
    to_chip, to_link = (frame + step, row), (other, row)
    row_sides = ((has_up, to_up, UP, DOWN), (has_down, to_down, DOWN, UP))

    def cols(c):
        return pl.ds(pl.multiple_of(c * wide, wide), wide)

    def head_cols(h):
        return pl.ds(pl.multiple_of(h * width, width), width)

    local = [
        pltpu.make_async_copy(src, dst, in_sem.at[i])
        for i, (src, dst) in enumerate(
            ((o_in, outs), (g_in, gs.at[OWN]), (q_in, qs.at[OWN]), (k_in, ks.at[0]), (v_in, vs.at[0]))
        )
    ]
    for copy in local:
        copy.start()

    barrier = pltpu.get_barrier_semaphore()
    pl.semaphore_signal(barrier, inc=1, device_id=to_chip, device_id_type=MESH)
    for there, dst in ((has_up, to_up), (has_down, to_down), (has_link, to_link)):
        @pl.when(there)
        def _():
            pl.semaphore_signal(barrier, inc=1, device_id=dst, device_id_type=MESH)
    peers = 1 + sum(there.astype(jnp.int32) for there in (has_up, has_down, has_link))
    pl.semaphore_wait(barrier, peers)

    def remote(src, dst, ss, rs, target):
        return pltpu.make_async_remote_copy(
            src_ref=src, dst_ref=dst, send_sem=ss, recv_sem=rs,
            device_id=target, device_id_type=MESH,
        )

    def query_copies(side, slot_there, target, c):
        return (
            remote(q_in.at[:, cols(c)], qs.at[slot_there, :, cols(c)], q_ss.at[side - 1, 0, c], q_rs.at[slot_there - 1, 0, c], target),
            remote(g_in.at[:, cols(c)], gs.at[slot_there, :, cols(c)], q_ss.at[side - 1, 1, c], q_rs.at[slot_there - 1, 1, c], target),
        )

    def aux_copy(side, slot_there, target):
        return remote(aux.at[OWN], aux.at[slot_there], aux_ss.at[side - 1], aux_rs.at[slot_there - 1], target)

    def key_copies(slot, target, c):
        return (
            remote(k_in.at[:, cols(c)], ks.at[slot, :, cols(c)], kv_ss.at[slot - 1, 0, c], kv_rs.at[slot - 1, 0, c], target),
            remote(v_in.at[:, cols(c)], vs.at[slot, :, cols(c)], kv_ss.at[slot - 1, 1, c], kv_rs.at[slot - 1, 1, c], target),
        )

    def dq_copy(side, slot_there, target, c):
        return remote(
            dq_send.at[side - 1, :, cols(c)], dq_recv.at[slot_there - 1, :, cols(c)],
            dq_ss.at[side - 1, c], dq_rs.at[slot_there - 1, c], target,
        )

    def dkv_copies(slot, target, c):
        return (
            remote(dk_send.at[slot - 1, :, cols(c)], dk_recv.at[slot - 1, :, cols(c)], dkv_ss.at[slot - 1, 0, c], dkv_rs.at[slot - 1, 0, c], target),
            remote(dv_send.at[slot - 1, :, cols(c)], dv_recv.at[slot - 1, :, cols(c)], dkv_ss.at[slot - 1, 1, c], dkv_rs.at[slot - 1, 1, c], target),
        )

    def loop(first, last, body):
        def run(c, carry):
            body(c)
            return carry

        lax.fori_loop(first, last, run, 0)

    def start_queries(c):
        for there, target, side, slot_there in row_sides:
            @pl.when(there)
            def _():
                for copy in query_copies(side, slot_there, target, c):
                    copy.start()

    def start_keys(c):
        for copy in key_copies(CHIP, to_chip, c):
            copy.start()
        @pl.when(has_link)
        def _():
            for copy in key_copies(LINK, to_link, c):
                copy.start()

    loop(0, EARLY, start_queries)
    loop(0, chunks, start_keys)

    local[0].wait()
    local[1].wait()
    aux[OWN] = jnp.zeros((AUX_ROWS, tile), F32)
    aux[OWN, 0:heads, :] = lse_ref[...] * LOG2E
    ones = jnp.ones((8, width), LOW)

    def delta_row(h):
        products = gs[OWN, :, head_cols(h)].astype(F32) * outs[:, head_cols(h)].astype(F32)
        high = products.astype(LOW)
        low = (products - high.astype(F32)).astype(LOW)
        aux[OWN, pl.ds(DELTA_ROW + h, 1), :] = (dot(ones, high, NT) + dot(ones, low, NT))[0:1]

    loop(0, heads, delta_row)
    for i in range(9):
        if i == 4:
            line = jnp.zeros((1, tile), F32)
        else:
            line = jnp.where(jnp.full((1, tile), mask_ref[0, i], jnp.int32) > 0, 0.0, 1e30)
        aux[OWN, PEN_ROW + i : PEN_ROW + i + 1, :] = line
    for there, target, side, slot_there in row_sides:
        @pl.when(there)
        def _():
            aux_copy(side, slot_there, target).start()
    loop(EARLY, chunks, start_queries)

    for there, slot in ((has_up, UP), (has_down, DOWN)):
        @pl.when(jnp.logical_not(there))
        def _():
            qs[slot] = jnp.zeros((tile, full), LOW)
            gs[slot] = jnp.zeros((tile, full), LOW)
            aux[slot] = jnp.zeros((AUX_ROWS, tile), F32)

    for copy in local[2:]:
        copy.wait()
    for there, target, side, slot_there in row_sides:
        @pl.when(there)
        def _():
            aux_copy(slot_there, side, target).wait_recv()

    def pick(source, first, index):
        table = aux[source, first : first + 16, :]
        chosen = lax.broadcasted_iota(jnp.int32, table.shape, 0) == index
        return jnp.sum(jnp.where(chosen, table, 0.0), 0, keepdims=True)

    def pair_block(h, slot, offset):
        at = head_cols(h)
        q = qs[:, :, at].reshape(3 * tile, width)
        g = gs[:, :, at].reshape(3 * tile, width)
        k, v = ks[slot, :, at], vs[slot, :, at]
        lines, deltas = [], []
        for source, row_offset in ((OWN, 0), (UP, -1), (DOWN, 1)):
            pen = 3 * (offset + 1) + row_offset + 1
            lines.append(pick(source, 0, h) + pick(source, PEN_ROW, pen))
            deltas.append(pick(source, DELTA_ROW, h))
        line, delta = jnp.concatenate(lines, 1), jnp.concatenate(deltas, 1)
        weights = jnp.exp2(dot(k, q, NT) * (scale * LOG2E) - line)
        grad_score = (weights * (dot(v, g, NT) - delta)).astype(LOW)
        dk = dot(grad_score, q, NN) * scale
        dv = dot(weights.astype(LOW), g, NN)
        return dk, dv, dot(k, grad_score, TN)

    def finish_queries(h, total):
        at = head_cols(h)
        for source in (OWN, UP, DOWN):
            part = total[:, source * tile : (source + 1) * tile].T * scale
            if source == OWN:
                dq_own[:, at] = part
            else:
                dq_send[source - 1, :, at] = part.astype(LOW)

    def start_dq(c):
        for there, target, side, slot_there in row_sides:
            @pl.when(there)
            def _():
                dq_copy(side, slot_there, target, c).start()

    def first_pass(c):
        for there, target, side, slot_there in row_sides:
            @pl.when(there)
            def _():
                for copy in query_copies(slot_there, side, target, c):
                    copy.wait_recv()
        for copy in key_copies(CHIP, to_chip, c):
            copy.wait_recv()
        for i in range(GROUP):
            h = c * GROUP + i
            at = head_cols(h)
            dk, dv, total = pair_block(h, 0, 0)
            dk_own[:, at] = dk
            dv_own[:, at] = dv
            dk, dv, more = pair_block(h, CHIP, step)
            dk_send[CHIP - 1, :, at] = dk.astype(LOW)
            dv_send[CHIP - 1, :, at] = dv.astype(LOW)
            total = total + more
            dq_acc[h] = total
            @pl.when(jnp.logical_not(has_link))
            def _():
                finish_queries(h, dq_acc[h])
        for copy in dkv_copies(CHIP, to_chip, c):
            copy.start()
        @pl.when(jnp.logical_not(has_link))
        def _():
            start_dq(c)

    loop(0, chunks, first_pass)

    def second_pass(c):
        for copy in key_copies(LINK, to_link, c):
            copy.wait_recv()
        for i in range(GROUP):
            h = c * GROUP + i
            at = head_cols(h)
            dk, dv, more = pair_block(h, LINK, -step)
            dk_send[LINK - 1, :, at] = dk.astype(LOW)
            dv_send[LINK - 1, :, at] = dv.astype(LOW)
            finish_queries(h, dq_acc[h] + more)
        for copy in dkv_copies(LINK, to_link, c):
            copy.start()
        start_dq(c)

    @pl.when(has_link)
    def _():
        loop(0, chunks, second_pass)

    @pl.when(jnp.logical_not(has_link))
    def _():
        dk_recv[LINK - 1] = jnp.zeros((tile, full), LOW)
        dv_recv[LINK - 1] = jnp.zeros((tile, full), LOW)
    for there, slot in ((has_up, UP), (has_down, DOWN)):
        @pl.when(jnp.logical_not(there))
        def _():
            dq_recv[slot - 1] = jnp.zeros((tile, full), LOW)

    def last_pass(c):
        at = cols(c)
        for there, target, side, slot_there in row_sides:
            @pl.when(there)
            def _():
                dq_copy(slot_there, side, target, c).wait_recv()
        for copy in dkv_copies(CHIP, to_chip, c):
            copy.wait_recv()
        @pl.when(has_link)
        def _():
            for copy in dkv_copies(LINK, to_link, c):
                copy.wait_recv()
        for own, recv, out in ((dq_own, dq_recv, dq_out), (dk_own, dk_recv, dk_out), (dv_own, dv_recv, dv_out)):
            out[:, at] = (own[:, at] + recv[0, :, at].astype(F32) + recv[1, :, at].astype(F32)).astype(LOW)

    loop(0, chunks, last_pass)

    for there, target, side, slot_there in row_sides:
        @pl.when(there)
        def _():
            aux_copy(side, slot_there, target).wait_send()

    def drain(c):
        for there, target, side, slot_there in row_sides:
            @pl.when(there)
            def _():
                for copy in query_copies(side, slot_there, target, c):
                    copy.wait_send()
                dq_copy(side, slot_there, target, c).wait_send()
        for copy in key_copies(CHIP, to_chip, c) + dkv_copies(CHIP, to_chip, c):
            copy.wait_send()
        @pl.when(has_link)
        def _():
            for copy in key_copies(LINK, to_link, c) + dkv_copies(LINK, to_link, c):
                copy.wait_send()

    loop(0, chunks, drain)


def per_device(queries, keys, values, outputs, out_grads, log_sums, window_mask):
    shape = queries.shape
    tile, full = shape[2:]
    heads = log_sums.shape[2]
    width = full // heads
    chunks = heads // GROUP
    flat = (tile, full)
    any_spec = pl.BlockSpec(memory_space=pl.ANY)
    vmem = pl.BlockSpec(memory_space=pltpu.VMEM)
    dma = pltpu.SemaphoreType.DMA
    grads = pl.pallas_call(
        kernel,
        out_shape=(jax.ShapeDtypeStruct(flat, LOW),) * 3,
        in_specs=[any_spec] * 5 + [vmem, pl.BlockSpec(memory_space=pltpu.SMEM)],
        out_specs=(vmem,) * 3,
        scratch_shapes=[
            *[pltpu.VMEM((3,) + flat, LOW)] * 4,
            pltpu.VMEM(flat, LOW),
            pltpu.VMEM((3, AUX_ROWS, tile), F32),
            pltpu.VMEM((heads, width, 3 * tile), F32),
            *[pltpu.VMEM(flat, F32)] * 3,
            *[pltpu.VMEM((2,) + flat, LOW)] * 6,
            dma((5,)),
            dma((2, 2, chunks)), dma((2, 2, chunks)),
            dma((2, 2, chunks)), dma((2, 2, chunks)),
            dma((2,)), dma((2,)),
            dma((2, chunks)), dma((2, chunks)),
            dma((2, 2, chunks)), dma((2, 2, chunks)),
        ],
        compiler_params=pltpu.CompilerParams(
            collective_id=0, has_side_effects=True, vmem_limit_bytes=63 * 2**20
        ),
        name="tile_attention_backward",
    )(
        *[x.reshape(flat) for x in (queries, keys, values, outputs, out_grads)],
        log_sums.reshape(heads, tile),
        window_mask.reshape(1, -1),
    )
    return tuple(g.reshape(shape) for g in grads)


def solution(mesh):
    tiles = P("tm", "space", None, None)
    return jax.shard_map(
        per_device,
        mesh=mesh,
        in_specs=(tiles,) * 6 + (P("tm", "space", None),),
        out_specs=(tiles,) * 3,
        check_vma=False,
    )
```

```python
import functools
import math

import jax
import jax.numpy as jnp
from jax import lax
from jax.experimental import pallas as pl
from jax.experimental.pallas import tpu as pltpu
from jax.sharding import PartitionSpec as P

F32 = jnp.float32
LOW = jnp.bfloat16
MESH = pl.DeviceIdType.MESH
GROUP = 1
EARLY = 2
LOG2E = math.log2(math.e)
NT = (((1,), (1,)), ((), ()))
NN = (((1,), (0,)), ((), ()))
TN = (((0,), (0,)), ((), ()))
OWN, UP, DOWN = 0, 1, 2
CHIP, LINK = 1, 2
DELTA_ROW, PEN_ROW, AUX_ROWS = 16, 32, 48
RELAYED = 6


def dot(a, b, dims):
    return lax.dot_general(a, b, dims, preferred_element_type=F32)


def kernel(
    q_in, k_in, v_in, o_in, g_in, lse_ref, mask_ref,
    dq_out, dk_out, dv_out,
    qs, gs, ks, vs, outs, aux, dq_acc, dq_own, dk_own, dv_own,
    dq_send, dk_send, dv_send, dq_recv, dk_recv, dv_recv, passing,
    in_sem, pass_rs, pass_ss, q_ss, q_rs, kv_ss, kv_rs, aux_ss, aux_rs, dq_ss, dq_rs, dkv_ss, dkv_rs,
):
    tile, full = q_in.shape
    heads = lse_ref.shape[0]
    width = full // heads
    wide = GROUP * width
    chunks = heads // GROUP
    scale = width**-0.5
    frame, row = lax.axis_index("tm"), lax.axis_index("space")
    frames, rows = lax.axis_size("tm"), lax.axis_size("space")
    odd = lax.rem(frame, 2)
    step = 1 - 2 * odd
    has_up, has_down = row < rows - 1, row > 0
    other = frame - step
    has_link = jnp.logical_and(other >= 0, other < frames)
    to_up, to_down = (frame, row + 1), (frame, row - 1)
    to_chip, to_link = (frame + step, row), (other, row)
    place = lax.rem(row, 4)
    partner = row + 1 - 2 * lax.rem(place, 2)
    is_outer = jnp.logical_or(place == 0, place == 3)
    via = jnp.logical_and(has_link, is_outer)
    carries = jnp.logical_and(has_link, jnp.logical_not(is_outer))
    to_partner, to_cross = (frame, partner), (other, partner)
    row_sides = ((has_up, to_up, UP, DOWN), (has_down, to_down, DOWN, UP))

    def cols(c):
        return pl.ds(pl.multiple_of(c * wide, wide), wide)

    def head_cols(h):
        return pl.ds(pl.multiple_of(h * width, width), width)

    local = [
        pltpu.make_async_copy(src, dst, in_sem.at[i])
        for i, (src, dst) in enumerate(
            ((o_in, outs), (g_in, gs.at[OWN]), (q_in, qs.at[OWN]), (k_in, ks.at[0]), (v_in, vs.at[0]))
        )
    ]
    for copy in local:
        copy.start()

    barrier = pltpu.get_barrier_semaphore()
    pl.semaphore_signal(barrier, inc=1, device_id=to_chip, device_id_type=MESH)
    for there, dst in ((has_up, to_up), (has_down, to_down), (has_link, to_link), (has_link, to_cross)):
        @pl.when(there)
        def _():
            pl.semaphore_signal(barrier, inc=1, device_id=dst, device_id_type=MESH)
    peers = 1 + sum(there.astype(jnp.int32) for there in (has_up, has_down, has_link, has_link))
    pl.semaphore_wait(barrier, peers)

    def remote(src, dst, ss, rs, target):
        return pltpu.make_async_remote_copy(
            src_ref=src, dst_ref=dst, send_sem=ss, recv_sem=rs,
            device_id=target, device_id_type=MESH,
        )

    def query_copies(side, slot_there, target, c):
        return (
            remote(q_in.at[:, cols(c)], qs.at[slot_there, :, cols(c)], q_ss.at[side - 1, 0, c], q_rs.at[slot_there - 1, 0, c], target),
            remote(g_in.at[:, cols(c)], gs.at[slot_there, :, cols(c)], q_ss.at[side - 1, 1, c], q_rs.at[slot_there - 1, 1, c], target),
        )

    def aux_copy(side, slot_there, target):
        return remote(aux.at[OWN], aux.at[slot_there], aux_ss.at[side - 1], aux_rs.at[slot_there - 1], target)

    def key_copies(slot, target, c):
        return (
            remote(k_in.at[:, cols(c)], ks.at[slot, :, cols(c)], kv_ss.at[slot - 1, 0, c], kv_rs.at[slot - 1, 0, c], target),
            remote(v_in.at[:, cols(c)], vs.at[slot, :, cols(c)], kv_ss.at[slot - 1, 1, c], kv_rs.at[slot - 1, 1, c], target),
        )

    def dq_copy(side, slot_there, target, c):
        return remote(
            dq_send.at[side - 1, :, cols(c)], dq_recv.at[slot_there - 1, :, cols(c)],
            dq_ss.at[side - 1, c], dq_rs.at[slot_there - 1, c], target,
        )

    def dkv_copies(slot, target, c):
        return (
            remote(dk_send.at[slot - 1, :, cols(c)], dk_recv.at[slot - 1, :, cols(c)], dkv_ss.at[slot - 1, 0, c], dkv_rs.at[slot - 1, 0, c], target),
            remote(dv_send.at[slot - 1, :, cols(c)], dv_recv.at[slot - 1, :, cols(c)], dkv_ss.at[slot - 1, 1, c], dkv_rs.at[slot - 1, 1, c], target),
        )

    def via_copies(kind, c):
        sources, ss = (((k_in, v_in), kv_ss), ((dk_send.at[LINK - 1], dv_send.at[LINK - 1]), dkv_ss))[kind]
        return [
            remote(src.at[:, cols(c)], passing.at[kind, i, :, cols(c)], ss.at[LINK - 1, i, c], pass_rs.at[kind, i, c], to_partner)
            for i, src in enumerate(sources)
        ]

    def onward_copies(kind, c):
        targets, rs = (((ks.at[LINK], vs.at[LINK]), kv_rs), ((dk_recv.at[LINK - 1], dv_recv.at[LINK - 1]), dkv_rs))[kind]
        return [
            remote(passing.at[kind, i, :, cols(c)], dst.at[:, cols(c)], pass_ss.at[kind, i, c], rs.at[LINK - 1, i, c], to_cross)
            for i, dst in enumerate(targets)
        ]

    def carry(kind, c):
        for copy in via_copies(kind, c):
            copy.wait_recv()
        for copy in onward_copies(kind, c):
            copy.start()

    def loop(first, last, body):
        def run(c, carry):
            body(c)
            return carry

        lax.fori_loop(first, last, run, 0)

    def start_queries(c):
        for there, target, side, slot_there in row_sides:
            @pl.when(there)
            def _():
                for copy in query_copies(side, slot_there, target, c):
                    copy.start()
        @pl.when(jnp.logical_and(via, jnp.logical_and(lax.rem(c, 2) == 1, c // 2 < RELAYED)))
        def _():
            for copy in via_copies(0, c // 2):
                copy.start()

    def start_keys(c):
        for copy in key_copies(CHIP, to_chip, c):
            copy.start()
        @pl.when(jnp.logical_and(has_link, jnp.logical_or(c >= RELAYED, carries)))
        def _():
            for copy in key_copies(LINK, to_link, c):
                copy.start()

    loop(0, EARLY, start_queries)
    loop(0, chunks, start_keys)

    local[0].wait()
    local[1].wait()
    aux[OWN] = jnp.zeros((AUX_ROWS, tile), F32)
    aux[OWN, 0:heads, :] = lse_ref[...] * LOG2E
    ones = jnp.ones((8, width), LOW)

    def delta_row(h):
        products = gs[OWN, :, head_cols(h)].astype(F32) * outs[:, head_cols(h)].astype(F32)
        high = products.astype(LOW)
        low = (products - high.astype(F32)).astype(LOW)
        aux[OWN, pl.ds(DELTA_ROW + h, 1), :] = (dot(ones, high, NT) + dot(ones, low, NT))[0:1]

    loop(0, heads, delta_row)
    for i in range(9):
        if i == 4:
            line = jnp.zeros((1, tile), F32)
        else:
            line = jnp.where(jnp.full((1, tile), mask_ref[0, i], jnp.int32) > 0, 0.0, 1e30)
        aux[OWN, PEN_ROW + i : PEN_ROW + i + 1, :] = line
    for there, target, side, slot_there in row_sides:
        @pl.when(there)
        def _():
            aux_copy(side, slot_there, target).start()
    loop(EARLY, chunks, start_queries)

    for there, slot in ((has_up, UP), (has_down, DOWN)):
        @pl.when(jnp.logical_not(there))
        def _():
            qs[slot] = jnp.zeros((tile, full), LOW)
            gs[slot] = jnp.zeros((tile, full), LOW)
            aux[slot] = jnp.zeros((AUX_ROWS, tile), F32)

    for copy in local[2:]:
        copy.wait()
    for there, target, side, slot_there in row_sides:
        @pl.when(there)
        def _():
            aux_copy(slot_there, side, target).wait_recv()

    def pick(source, first, index):
        table = aux[source, first : first + 16, :]
        chosen = lax.broadcasted_iota(jnp.int32, table.shape, 0) == index
        return jnp.sum(jnp.where(chosen, table, 0.0), 0, keepdims=True)

    def pair_block(h, slot, offset):
        at = head_cols(h)
        q = qs[:, :, at].reshape(3 * tile, width)
        g = gs[:, :, at].reshape(3 * tile, width)
        k, v = ks[slot, :, at], vs[slot, :, at]
        lines, deltas = [], []
        for source, row_offset in ((OWN, 0), (UP, -1), (DOWN, 1)):
            pen = 3 * (offset + 1) + row_offset + 1
            lines.append(pick(source, 0, h) + pick(source, PEN_ROW, pen))
            deltas.append(pick(source, DELTA_ROW, h))
        line, delta = jnp.concatenate(lines, 1), jnp.concatenate(deltas, 1)
        weights = jnp.exp2(dot(k, q, NT) * (scale * LOG2E) - line)
        grad_score = (weights * (dot(v, g, NT) - delta)).astype(LOW)
        dk = dot(grad_score, q, NN) * scale
        dv = dot(weights.astype(LOW), g, NN)
        return dk, dv, dot(k, grad_score, TN)

    def finish_queries(h, total):
        at = head_cols(h)
        for source in (OWN, UP, DOWN):
            part = total[:, source * tile : (source + 1) * tile].T * scale
            if source == OWN:
                dq_own[:, at] = part
            else:
                dq_send[source - 1, :, at] = part.astype(LOW)

    def start_dq(c):
        for there, target, side, slot_there in row_sides:
            @pl.when(there)
            def _():
                dq_copy(side, slot_there, target, c).start()

    def first_pass(c):
        for there, target, side, slot_there in row_sides:
            @pl.when(there)
            def _():
                for copy in query_copies(slot_there, side, target, c):
                    copy.wait_recv()
        for copy in key_copies(CHIP, to_chip, c):
            copy.wait_recv()
        @pl.when(jnp.logical_and(carries, jnp.logical_and(lax.rem(c, 2) == 0, c >= 2)))
        def _():
            carry(0, c // 2 - 1)
        for i in range(GROUP):
            h = c * GROUP + i
            at = head_cols(h)
            dk, dv, total = pair_block(h, 0, 0)
            dk_own[:, at] = dk
            dv_own[:, at] = dv
            dk, dv, more = pair_block(h, CHIP, step)
            dk_send[CHIP - 1, :, at] = dk.astype(LOW)
            dv_send[CHIP - 1, :, at] = dv.astype(LOW)
            total = total + more
            dq_acc[h] = total
            @pl.when(jnp.logical_not(has_link))
            def _():
                finish_queries(h, dq_acc[h])
        for copy in dkv_copies(CHIP, to_chip, c):
            copy.start()
        @pl.when(jnp.logical_not(has_link))
        def _():
            start_dq(c)

    loop(0, chunks, first_pass)

    @pl.when(carries)
    def _():
        carry(0, RELAYED - 1)

    def second_pass(c):
        for copy in key_copies(LINK, to_link, c):
            copy.wait_recv()
        for i in range(GROUP):
            h = c * GROUP + i
            at = head_cols(h)
            dk, dv, more = pair_block(h, LINK, -step)
            dk_send[LINK - 1, :, at] = dk.astype(LOW)
            dv_send[LINK - 1, :, at] = dv.astype(LOW)
            finish_queries(h, dq_acc[h] + more)
        relayed = jnp.logical_and(is_outer, c < RELAYED)
        @pl.when(relayed)
        def _():
            for copy in via_copies(1, c):
                copy.start()
        @pl.when(jnp.logical_not(relayed))
        def _():
            for copy in dkv_copies(LINK, to_link, c):
                copy.start()
        start_dq(c)

    @pl.when(has_link)
    def _():
        loop(0, chunks, second_pass)

    @pl.when(carries)
    def _():
        loop(0, RELAYED, lambda c: carry(1, c))

    @pl.when(jnp.logical_not(has_link))
    def _():
        dk_recv[LINK - 1] = jnp.zeros((tile, full), LOW)
        dv_recv[LINK - 1] = jnp.zeros((tile, full), LOW)
    for there, slot in ((has_up, UP), (has_down, DOWN)):
        @pl.when(jnp.logical_not(there))
        def _():
            dq_recv[slot - 1] = jnp.zeros((tile, full), LOW)

    def last_pass(c):
        at = cols(c)
        for there, target, side, slot_there in row_sides:
            @pl.when(there)
            def _():
                dq_copy(slot_there, side, target, c).wait_recv()
        for copy in dkv_copies(CHIP, to_chip, c):
            copy.wait_recv()
        @pl.when(has_link)
        def _():
            for copy in dkv_copies(LINK, to_link, c):
                copy.wait_recv()
        for own, recv, out in ((dq_own, dq_recv, dq_out), (dk_own, dk_recv, dk_out), (dv_own, dv_recv, dv_out)):
            out[:, at] = (own[:, at] + recv[0, :, at].astype(F32) + recv[1, :, at].astype(F32)).astype(LOW)

    loop(0, chunks, last_pass)

    for there, target, side, slot_there in row_sides:
        @pl.when(there)
        def _():
            aux_copy(side, slot_there, target).wait_send()

    def drain(c):
        for there, target, side, slot_there in row_sides:
            @pl.when(there)
            def _():
                for copy in query_copies(side, slot_there, target, c):
                    copy.wait_send()
                dq_copy(side, slot_there, target, c).wait_send()
        for copy in key_copies(CHIP, to_chip, c) + dkv_copies(CHIP, to_chip, c):
            copy.wait_send()
        @pl.when(has_link)
        def _():
            for copy in key_copies(LINK, to_link, c) + dkv_copies(LINK, to_link, c):
                copy.wait_send()

    loop(0, chunks, drain)

    def drain_carried(c):
        for kind in (0, 1):
            for copy in onward_copies(kind, c):
                copy.wait_send()

    @pl.when(carries)
    def _():
        loop(0, RELAYED, drain_carried)


def per_device(queries, keys, values, outputs, out_grads, log_sums, window_mask):
    shape = queries.shape
    tile, full = shape[2:]
    heads = log_sums.shape[2]
    width = full // heads
    chunks = heads // GROUP
    flat = (tile, full)
    any_spec = pl.BlockSpec(memory_space=pl.ANY)
    vmem = pl.BlockSpec(memory_space=pltpu.VMEM)
    dma = pltpu.SemaphoreType.DMA
    grads = pl.pallas_call(
        kernel,
        out_shape=(jax.ShapeDtypeStruct(flat, LOW),) * 3,
        in_specs=[any_spec] * 5 + [vmem, pl.BlockSpec(memory_space=pltpu.SMEM)],
        out_specs=(vmem,) * 3,
        scratch_shapes=[
            *[pltpu.VMEM((3,) + flat, LOW)] * 4,
            pltpu.VMEM(flat, LOW),
            pltpu.VMEM((3, AUX_ROWS, tile), F32),
            pltpu.VMEM((heads, width, 3 * tile), F32),
            *[pltpu.VMEM(flat, F32)] * 3,
            *[pltpu.VMEM((2,) + flat, LOW)] * 6,
            pltpu.VMEM((2, 2, tile, RELAYED * GROUP * width), LOW),
            dma((5,)), dma((2, 2, RELAYED)), dma((2, 2, RELAYED)),
            dma((2, 2, chunks)), dma((2, 2, chunks)),
            dma((2, 2, chunks)), dma((2, 2, chunks)),
            dma((2,)), dma((2,)),
            dma((2, chunks)), dma((2, chunks)),
            dma((2, 2, chunks)), dma((2, 2, chunks)),
        ],
        compiler_params=pltpu.CompilerParams(
            collective_id=0, has_side_effects=True, vmem_limit_bytes=63 * 2**20
        ),
        name="tile_attention_backward",
    )(
        *[x.reshape(flat) for x in (queries, keys, values, outputs, out_grads)],
        log_sums.reshape(heads, tile),
        window_mask.reshape(1, -1),
    )
    return tuple(g.reshape(shape) for g in grads)


def solution(mesh):
    tiles = P("tm", "space", None, None)
    return jax.shard_map(
        per_device,
        mesh=mesh,
        in_specs=(tiles,) * 6 + (P("tm", "space", None),),
        out_specs=(tiles,) * 3,
        check_vma=False,
    )
```

```python
import functools
import math

import jax
import jax.numpy as jnp
from jax import lax
from jax.experimental import pallas as pl
from jax.experimental.pallas import tpu as pltpu
from jax.sharding import PartitionSpec as P

F32 = jnp.float32
LOW = jnp.bfloat16
MESH = pl.DeviceIdType.MESH
GROUP = 1
EARLY = 2
LOG2E = math.log2(math.e)
NT = (((1,), (1,)), ((), ()))
NN = (((1,), (0,)), ((), ()))
TN = (((0,), (0,)), ((), ()))
OWN, UP, DOWN = 0, 1, 2
CHIP, LINK = 1, 2
DELTA_ROW, PEN_ROW, AUX_ROWS = 16, 32, 48
VIA_KEYS = 12
VIA_GRADS = 0
LEAD = 3


def dot(a, b, dims):
    return lax.dot_general(a, b, dims, preferred_element_type=F32)


def kernel(
    q_in, k_in, v_in, o_in, g_in, lse_ref, mask_ref,
    dq_out, dk_out, dv_out,
    qs, gs, ks, vs, outs, aux, dq_sum, dq_own, dk_own, dv_own,
    dq_send, dk_send, dv_send, dq_recv, dk_recv, dv_recv, passing,
    in_sem, pass_rs, pass_ss, q_ss, q_rs, kv_ss, kv_rs, aux_ss, aux_rs, dq_ss, dq_rs, dkv_ss, dkv_rs,
):
    tile, full = q_in.shape
    heads = lse_ref.shape[0]
    width = full // heads
    wide = GROUP * width
    chunks = heads // GROUP
    scale = width**-0.5
    frame, row = lax.axis_index("tm"), lax.axis_index("space")
    frames, rows = lax.axis_size("tm"), lax.axis_size("space")
    odd = lax.rem(frame, 2)
    step = 1 - 2 * odd
    has_up, has_down = row < rows - 1, row > 0
    other = frame - step
    has_link = jnp.logical_and(other >= 0, other < frames)
    to_up, to_down = (frame, row + 1), (frame, row - 1)
    to_chip, to_link = (frame + step, row), (other, row)
    place = lax.rem(row, 4)
    partner = row + 1 - 2 * lax.rem(place, 2)
    is_outer = jnp.logical_or(place == 0, place == 3)
    via = jnp.logical_and(has_link, is_outer)
    carries = jnp.logical_and(has_link, jnp.logical_not(is_outer))
    to_partner, to_cross = (frame, partner), (other, partner)
    row_sides = ((has_up, to_up, UP, DOWN), (has_down, to_down, DOWN, UP))

    def cols(c):
        return pl.ds(pl.multiple_of(c * wide, wide), wide)

    def head_cols(h):
        return pl.ds(pl.multiple_of(h * width, width), width)

    local = [
        pltpu.make_async_copy(src, dst, in_sem.at[i])
        for i, (src, dst) in enumerate(
            ((o_in, outs), (g_in, gs.at[OWN]), (q_in, qs.at[OWN]), (k_in, ks.at[0]), (v_in, vs.at[0]))
        )
    ]
    for copy in local:
        copy.start()

    barrier = pltpu.get_barrier_semaphore()
    pl.semaphore_signal(barrier, inc=1, device_id=to_chip, device_id_type=MESH)
    for there, dst in ((has_up, to_up), (has_down, to_down), (has_link, to_link), (has_link, to_cross)):
        @pl.when(there)
        def _():
            pl.semaphore_signal(barrier, inc=1, device_id=dst, device_id_type=MESH)
    peers = 1 + sum(there.astype(jnp.int32) for there in (has_up, has_down, has_link, has_link))
    pl.semaphore_wait(barrier, peers)

    def remote(src, dst, ss, rs, target):
        return pltpu.make_async_remote_copy(
            src_ref=src, dst_ref=dst, send_sem=ss, recv_sem=rs,
            device_id=target, device_id_type=MESH,
        )

    def query_copies(side, slot_there, target, c):
        return (
            remote(q_in.at[:, cols(c)], qs.at[slot_there, :, cols(c)], q_ss.at[side - 1, 0, c], q_rs.at[slot_there - 1, 0, c], target),
            remote(g_in.at[:, cols(c)], gs.at[slot_there, :, cols(c)], q_ss.at[side - 1, 1, c], q_rs.at[slot_there - 1, 1, c], target),
        )

    def aux_copy(side, slot_there, target):
        return remote(aux.at[OWN], aux.at[slot_there], aux_ss.at[side - 1], aux_rs.at[slot_there - 1], target)

    def key_copies(slot, target, c):
        return (
            remote(k_in.at[:, cols(c)], ks.at[slot, :, cols(c)], kv_ss.at[slot - 1, 0, c], kv_rs.at[slot - 1, 0, c], target),
            remote(v_in.at[:, cols(c)], vs.at[slot, :, cols(c)], kv_ss.at[slot - 1, 1, c], kv_rs.at[slot - 1, 1, c], target),
        )

    def dq_copy(side, slot_there, target, c):
        return remote(
            dq_send.at[side - 1, :, cols(c)], dq_recv.at[slot_there - 1, :, cols(c)],
            dq_ss.at[side - 1, c], dq_rs.at[slot_there - 1, c], target,
        )

    def dkv_copies(slot, target, c):
        return (
            remote(dk_send.at[slot - 1, :, cols(c)], dk_recv.at[slot - 1, :, cols(c)], dkv_ss.at[slot - 1, 0, c], dkv_rs.at[slot - 1, 0, c], target),
            remote(dv_send.at[slot - 1, :, cols(c)], dv_recv.at[slot - 1, :, cols(c)], dkv_ss.at[slot - 1, 1, c], dkv_rs.at[slot - 1, 1, c], target),
        )

    def via_copies(kind, c):
        sources, ss = (((k_in, v_in), kv_ss), ((dk_send.at[LINK - 1], dv_send.at[LINK - 1]), dkv_ss))[kind]
        return [
            remote(src.at[:, cols(c)], passing.at[kind, i, :, cols(c)], ss.at[LINK - 1, i, c], pass_rs.at[kind, i, c], to_partner)
            for i, src in enumerate(sources)
        ]

    def onward_copies(kind, c):
        targets, rs = (((ks.at[LINK], vs.at[LINK]), kv_rs), ((dk_recv.at[LINK - 1], dv_recv.at[LINK - 1]), dkv_rs))[kind]
        return [
            remote(passing.at[kind, i, :, cols(c)], dst.at[:, cols(c)], pass_ss.at[kind, i, c], rs.at[LINK - 1, i, c], to_cross)
            for i, dst in enumerate(targets)
        ]

    def carry(kind, c):
        for copy in via_copies(kind, c):
            copy.wait_recv()
        for copy in onward_copies(kind, c):
            copy.start()

    def loop(first, last, body):
        def run(c, carry):
            body(c)
            return carry

        lax.fori_loop(first, last, run, 0)

    def start_queries(c):
        @pl.when(jnp.logical_and(via, c < VIA_KEYS))
        def _():
            for copy in via_copies(0, c):
                copy.start()
        for there, target, side, slot_there in row_sides:
            @pl.when(there)
            def _():
                for copy in query_copies(side, slot_there, target, c):
                    copy.start()

    def start_keys(c):
        for copy in key_copies(CHIP, to_chip, c):
            copy.start()

    def start_link_keys(c):
        for copy in key_copies(LINK, to_link, c):
            copy.start()

    loop(0, EARLY, start_queries)
    loop(0, chunks, start_keys)

    @pl.when(carries)
    def _():
        loop(0, LEAD, start_link_keys)

    @pl.when(via)
    def _():
        loop(VIA_KEYS, chunks, start_link_keys)

    local[0].wait()
    local[1].wait()
    aux[OWN] = jnp.zeros((AUX_ROWS, tile), F32)
    aux[OWN, 0:heads, :] = lse_ref[...] * LOG2E
    ones = jnp.ones((8, width), LOW)

    def delta_row(h):
        products = gs[OWN, :, head_cols(h)].astype(F32) * outs[:, head_cols(h)].astype(F32)
        high = products.astype(LOW)
        low = (products - high.astype(F32)).astype(LOW)
        aux[OWN, pl.ds(DELTA_ROW + h, 1), :] = (dot(ones, high, NT) + dot(ones, low, NT))[0:1]

    loop(0, heads, delta_row)
    for i in range(9):
        if i == 4:
            line = jnp.zeros((1, tile), F32)
        else:
            line = jnp.where(jnp.full((1, tile), mask_ref[0, i], jnp.int32) > 0, 0.0, 1e30)
        aux[OWN, PEN_ROW + i : PEN_ROW + i + 1, :] = line
    for there, target, side, slot_there in row_sides:
        @pl.when(there)
        def _():
            aux_copy(side, slot_there, target).start()
    loop(EARLY, chunks, start_queries)

    for there, slot in ((has_up, UP), (has_down, DOWN)):
        @pl.when(jnp.logical_not(there))
        def _():
            qs[slot] = jnp.zeros((tile, full), LOW)
            gs[slot] = jnp.zeros((tile, full), LOW)
            aux[slot] = jnp.zeros((AUX_ROWS, tile), F32)

    for copy in local[2:]:
        copy.wait()
    for there, target, side, slot_there in row_sides:
        @pl.when(there)
        def _():
            aux_copy(slot_there, side, target).wait_recv()

    def pick(source, first, index):
        table = aux[source, first : first + 16, :]
        chosen = lax.broadcasted_iota(jnp.int32, table.shape, 0) == index
        return jnp.sum(jnp.where(chosen, table, 0.0), 0, keepdims=True)

    def pair_block(h, slot, offset):
        at = head_cols(h)
        q = qs[:, :, at].reshape(3 * tile, width)
        g = gs[:, :, at].reshape(3 * tile, width)
        k, v = ks[slot, :, at], vs[slot, :, at]
        lines, deltas = [], []
        for source, row_offset in ((OWN, 0), (UP, -1), (DOWN, 1)):
            pen = 3 * (offset + 1) + row_offset + 1
            lines.append(pick(source, 0, h) + pick(source, PEN_ROW, pen))
            deltas.append(pick(source, DELTA_ROW, h))
        line, delta = jnp.concatenate(lines, 1), jnp.concatenate(deltas, 1)
        weights = jnp.exp2(dot(k, q, NT) * (scale * LOG2E) - line)
        grad_score = (weights * (dot(v, g, NT) - delta)).astype(LOW)
        dk = dot(grad_score, q, NN) * scale
        dv = dot(weights.astype(LOW), g, NN)
        return dk, dv, dot(k, grad_score, TN)

    def finish_queries(h, total):
        at = head_cols(h)
        for source in (OWN, UP, DOWN):
            part = total[:, source * tile : (source + 1) * tile].T * scale
            if source == OWN:
                dq_own[:, at] = part
            else:
                dq_send[source - 1, :, at] = part.astype(LOW)

    def start_dq(c):
        for there, target, side, slot_there in row_sides:
            @pl.when(there)
            def _():
                dq_copy(side, slot_there, target, c).start()

    def compute(c):
        for there, target, side, slot_there in row_sides:
            @pl.when(there)
            def _():
                for copy in query_copies(slot_there, side, target, c):
                    copy.wait_recv()

        @pl.when(jnp.logical_and(carries, c < VIA_KEYS))
        def _():
            carry(0, c)

        @pl.when(jnp.logical_and(carries, c + LEAD < chunks))
        def _():
            start_link_keys(c + LEAD)

        for copy in key_copies(CHIP, to_chip, c):
            copy.wait_recv()
        for i in range(GROUP):
            h = c * GROUP + i
            at = head_cols(h)
            dk, dv, total = pair_block(h, 0, 0)
            dk_own[:, at] = dk
            dv_own[:, at] = dv
            dk, dv, more = pair_block(h, CHIP, step)
            dk_send[CHIP - 1, :, at] = dk.astype(LOW)
            dv_send[CHIP - 1, :, at] = dv.astype(LOW)
            dq_sum[...] = total + more
            if i == GROUP - 1:
                for copy in dkv_copies(CHIP, to_chip, c):
                    copy.start()

            @pl.when(has_link)
            def _():
                if i == 0:
                    for copy in key_copies(LINK, to_link, c):
                        copy.wait_recv()
                dk, dv, more = pair_block(h, LINK, -step)
                dk_send[LINK - 1, :, at] = dk.astype(LOW)
                dv_send[LINK - 1, :, at] = dv.astype(LOW)
                dq_sum[...] += more

            finish_queries(h, dq_sum[...])

        start_dq(c)
        relayed = jnp.logical_and(is_outer, c < VIA_GRADS)
        @pl.when(jnp.logical_and(has_link, relayed))
        def _():
            for copy in via_copies(1, c):
                copy.start()
        @pl.when(jnp.logical_and(has_link, jnp.logical_not(relayed)))
        def _():
            for copy in dkv_copies(LINK, to_link, c):
                copy.start()

    loop(0, chunks, compute)

    @pl.when(carries)
    def _():
        loop(0, VIA_GRADS, lambda c: carry(1, c))

    @pl.when(jnp.logical_not(has_link))
    def _():
        dk_recv[LINK - 1] = jnp.zeros((tile, full), LOW)
        dv_recv[LINK - 1] = jnp.zeros((tile, full), LOW)
    for there, slot in ((has_up, UP), (has_down, DOWN)):
        @pl.when(jnp.logical_not(there))
        def _():
            dq_recv[slot - 1] = jnp.zeros((tile, full), LOW)

    def last_pass(c):
        at = cols(c)
        for there, target, side, slot_there in row_sides:
            @pl.when(there)
            def _():
                dq_copy(slot_there, side, target, c).wait_recv()
        for copy in dkv_copies(CHIP, to_chip, c):
            copy.wait_recv()
        @pl.when(has_link)
        def _():
            for copy in dkv_copies(LINK, to_link, c):
                copy.wait_recv()
        for own, recv, out in ((dq_own, dq_recv, dq_out), (dk_own, dk_recv, dk_out), (dv_own, dv_recv, dv_out)):
            out[:, at] = (own[:, at] + recv[0, :, at].astype(F32) + recv[1, :, at].astype(F32)).astype(LOW)

    loop(0, chunks, last_pass)

    for there, target, side, slot_there in row_sides:
        @pl.when(there)
        def _():
            aux_copy(side, slot_there, target).wait_send()

    def drain(c):
        for there, target, side, slot_there in row_sides:
            @pl.when(there)
            def _():
                for copy in query_copies(side, slot_there, target, c):
                    copy.wait_send()
                dq_copy(side, slot_there, target, c).wait_send()
        for copy in key_copies(CHIP, to_chip, c) + dkv_copies(CHIP, to_chip, c):
            copy.wait_send()
        @pl.when(has_link)
        def _():
            for copy in key_copies(LINK, to_link, c) + dkv_copies(LINK, to_link, c):
                copy.wait_send()

    loop(0, chunks, drain)

    def drain_carried(kind):
        def run(c):
            for copy in onward_copies(kind, c):
                copy.wait_send()

        return run

    @pl.when(carries)
    def _():
        loop(0, VIA_KEYS, drain_carried(0))
        loop(0, VIA_GRADS, drain_carried(1))


def per_device(queries, keys, values, outputs, out_grads, log_sums, window_mask):
    shape = queries.shape
    tile, full = shape[2:]
    heads = log_sums.shape[2]
    width = full // heads
    chunks = heads // GROUP
    flat = (tile, full)
    any_spec = pl.BlockSpec(memory_space=pl.ANY)
    vmem = pl.BlockSpec(memory_space=pltpu.VMEM)
    dma = pltpu.SemaphoreType.DMA
    grads = pl.pallas_call(
        kernel,
        out_shape=(jax.ShapeDtypeStruct(flat, LOW),) * 3,
        in_specs=[any_spec] * 5 + [vmem, pl.BlockSpec(memory_space=pltpu.SMEM)],
        out_specs=(vmem,) * 3,
        scratch_shapes=[
            *[pltpu.VMEM((3,) + flat, LOW)] * 4,
            pltpu.VMEM(flat, LOW),
            pltpu.VMEM((3, AUX_ROWS, tile), F32),
            pltpu.VMEM((width, 3 * tile), F32),
            *[pltpu.VMEM(flat, F32)] * 3,
            *[pltpu.VMEM((2,) + flat, LOW)] * 6,
            pltpu.VMEM((2, 2) + flat, LOW),
            dma((5,)), dma((2, 2, chunks)), dma((2, 2, chunks)),
            dma((2, 2, chunks)), dma((2, 2, chunks)),
            dma((2, 2, chunks)), dma((2, 2, chunks)),
            dma((2,)), dma((2,)),
            dma((2, chunks)), dma((2, chunks)),
            dma((2, 2, chunks)), dma((2, 2, chunks)),
        ],
        compiler_params=pltpu.CompilerParams(
            collective_id=0, has_side_effects=True, vmem_limit_bytes=63 * 2**20
        ),
        name="tile_attention_backward",
    )(
        *[x.reshape(flat) for x in (queries, keys, values, outputs, out_grads)],
        log_sums.reshape(heads, tile),
        window_mask.reshape(1, -1),
    )
    return tuple(g.reshape(shape) for g in grads)


def solution(mesh):
    tiles = P("tm", "space", None, None)
    return jax.shard_map(
        per_device,
        mesh=mesh,
        in_specs=(tiles,) * 6 + (P("tm", "space", None),),
        out_specs=(tiles,) * 3,
        check_vma=False,
    )
```

```python
import functools
import math

import jax
import jax.numpy as jnp
from jax import lax
from jax.experimental import pallas as pl
from jax.experimental.pallas import tpu as pltpu
from jax.sharding import PartitionSpec as P

F32 = jnp.float32
LOW = jnp.bfloat16
MESH = pl.DeviceIdType.MESH
EARLY = 2
LOG2E = math.log2(math.e)
NT = (((1,), (1,)), ((), ()))
NN = (((1,), (0,)), ((), ()))
TN = (((0,), (0,)), ((), ()))
OWN, NEAR, ACROSS = 0, 1, 2
CHIP, LINK, FAR = 1, 2, 3
DELTA_ROW, PEN_ROW, AUX_ROWS = 12, 24, 40
VIA_KEYS = 3
VIA_GRADS = 0
LEAD = 3


def dot(a, b, dims):
    return lax.dot_general(a, b, dims, preferred_element_type=F32)


def kernel(
    q_in, k_in, v_in, o_in, g_in, lse_ref, mask_ref,
    dq_out, dk_out, dv_out,
    qs, gs, ks, vs, outs, aux, dq_sum, held, dq_own, dk_own, dv_own,
    dq_send, dk_send, dv_send, dq_recv, dk_recv, dv_recv, passing,
    in_sem, pass_rs, pass_ss, q_ss, q_rs, kv_ss, kv_rs, aux_ss, aux_rs, dq_ss, dq_rs, dkv_ss, dkv_rs,
):
    tile, full = q_in.shape
    heads = lse_ref.shape[0]
    width = full // heads
    wide, chunks = width, heads
    scale = width**-0.5
    frame, row = lax.axis_index("tm"), lax.axis_index("space")
    frames, rows = lax.axis_size("tm"), lax.axis_size("space")
    odd = lax.rem(frame, 2)
    step = 1 - 2 * odd
    place = lax.rem(row, 4)
    toward = 1 - 2 * lax.rem(place, 2)
    partner, beyond = row + toward, row - toward
    outer = jnp.logical_or(place == 0, place == 3)
    inner = jnp.logical_not(outer)
    other = frames - 1 - frame
    middle = jnp.abs(other - frame) == 1
    has_link = jnp.logical_or(outer, middle)
    has_across = jnp.logical_and(beyond >= 0, beyond < rows)
    across_frame = jnp.where(outer, other, frame)
    to_near, to_across = (frame, partner), (across_frame, beyond)
    to_chip, to_link, to_cross = (frame + step, row), (other, row), (other, partner)
    key_frames = (frame, frame + step, other, frames - 1 - (frame + step))
    query_frames = ((frame, 0), (frame, -toward), (across_frame, toward))

    def cols(c):
        return pl.ds(pl.multiple_of(c * wide, wide), wide)

    def head_cols(h):
        return pl.ds(pl.multiple_of(h * width, width), width)

    local = [
        pltpu.make_async_copy(src, dst, in_sem.at[i])
        for i, (src, dst) in enumerate(
            ((o_in, outs), (g_in, gs.at[OWN]), (q_in, qs.at[OWN]), (k_in, ks.at[0]), (v_in, vs.at[0]))
        )
    ]
    for copy in local:
        copy.start()

    barrier = pltpu.get_barrier_semaphore()
    pl.semaphore_signal(barrier, inc=1, device_id=to_chip, device_id_type=MESH)
    pl.semaphore_signal(barrier, inc=1, device_id=to_near, device_id_type=MESH)
    for there, dst in ((has_across, to_across), (has_link, to_link)):
        @pl.when(there)
        def _():
            pl.semaphore_signal(barrier, inc=1, device_id=dst, device_id_type=MESH)
    pl.semaphore_signal(barrier, inc=1, device_id=to_cross, device_id_type=MESH)
    peers = 3 + has_across.astype(jnp.int32) + has_link.astype(jnp.int32)
    pl.semaphore_wait(barrier, peers)

    def remote(src, dst, ss, rs, target):
        return pltpu.make_async_remote_copy(
            src_ref=src, dst_ref=dst, send_sem=ss, recv_sem=rs,
            device_id=target, device_id_type=MESH,
        )

    def query_copies(slot, c):
        target = to_near if slot == NEAR else to_across
        return [
            remote(src.at[:, cols(c)], dst.at[slot, :, cols(c)], q_ss.at[slot - 1, i, c], q_rs.at[slot - 1, i, c], target)
            for i, (src, dst) in enumerate(((q_in, qs), (g_in, gs)))
        ]

    def aux_copy(slot):
        target = to_near if slot == NEAR else to_across
        return remote(aux.at[OWN], aux.at[slot], aux_ss.at[slot - 1], aux_rs.at[slot - 1], target)

    def key_copies(slot, target, c):
        sources = (ks.at[LINK], vs.at[LINK]) if slot == FAR else (k_in, v_in)
        return [
            remote(src.at[:, cols(c)], dst.at[slot, :, cols(c)], kv_ss.at[slot - 1, i, c], kv_rs.at[slot - 1, i, c], target)
            for i, (src, dst) in enumerate(zip(sources, (ks, vs)))
        ]

    def dq_copy(slot, c):
        target = to_near if slot == NEAR else to_across
        return remote(
            dq_send.at[slot - 1, :, cols(c)], dq_recv.at[slot - 1, :, cols(c)],
            dq_ss.at[slot - 1, c], dq_rs.at[slot - 1, c], target,
        )

    def dkv_copies(slot, target, c):
        return (
            remote(dk_send.at[slot - 1, :, cols(c)], dk_recv.at[slot - 1, :, cols(c)], dkv_ss.at[slot - 1, 0, c], dkv_rs.at[slot - 1, 0, c], target),
            remote(dv_send.at[slot - 1, :, cols(c)], dv_recv.at[slot - 1, :, cols(c)], dkv_ss.at[slot - 1, 1, c], dkv_rs.at[slot - 1, 1, c], target),
        )

    def via_copies(kind, c):
        sources, ss = (((k_in, v_in), kv_ss), ((dk_send.at[LINK - 1], dv_send.at[LINK - 1]), dkv_ss))[kind]
        return [
            remote(src.at[:, cols(c)], passing.at[kind, i, :, cols(c)], ss.at[LINK - 1, i, c], pass_rs.at[kind, i, c], to_near)
            for i, src in enumerate(sources)
        ]

    def onward_copies(kind, c):
        targets, rs = (((ks.at[LINK], vs.at[LINK]), kv_rs), ((dk_recv.at[LINK - 1], dv_recv.at[LINK - 1]), dkv_rs))[kind]
        return [
            remote(passing.at[kind, i, :, cols(c)], dst.at[:, cols(c)], pass_ss.at[kind, i, c], rs.at[LINK - 1, i, c], to_cross)
            for i, dst in enumerate(targets)
        ]

    def carry(kind, c):
        for copy in via_copies(kind, c):
            copy.wait_recv()
        for copy in onward_copies(kind, c):
            copy.start()

    def loop(first, last, body):
        def run(c, carry):
            body(c)
            return carry

        lax.fori_loop(first, last, run, 0)

    def start_queries(c):
        @pl.when(jnp.logical_and(outer, c < VIA_KEYS))
        def _():
            for copy in via_copies(0, c):
                copy.start()
        for copy in query_copies(NEAR, c):
            copy.start()

        @pl.when(has_across)
        def _():
            for copy in query_copies(ACROSS, c):
                copy.start()

    def start_keys(c):
        for copy in key_copies(CHIP, to_chip, c):
            copy.start()

    def start_link_keys(c):
        for copy in key_copies(LINK, to_link, c):
            copy.start()

    loop(0, EARLY, start_queries)
    loop(0, chunks, start_keys)

    @pl.when(jnp.logical_and(inner, has_link))
    def _():
        loop(0, LEAD, start_link_keys)

    @pl.when(outer)
    def _():
        loop(VIA_KEYS, chunks, start_link_keys)

    local[0].wait()
    local[1].wait()
    aux[OWN] = jnp.zeros((AUX_ROWS, tile), F32)
    for h in range(heads):
        aux[OWN, h : h + 1, :] = lse_ref[h] * LOG2E
    ones = jnp.ones((8, width), LOW)

    def delta_row(h):
        products = gs[OWN, :, head_cols(h)].astype(F32) * outs[:, head_cols(h)].astype(F32)
        high = products.astype(LOW)
        low = (products - high.astype(F32)).astype(LOW)
        aux[OWN, pl.ds(DELTA_ROW + h, 1), :] = (dot(ones, high, NT) + dot(ones, low, NT))[0:1]

    loop(0, heads, delta_row)
    for i in range(9):
        if i == 4:
            line = jnp.zeros((1, tile), F32)
        else:
            line = jnp.where(jnp.full((1, tile), mask_ref[0, i], jnp.int32) > 0, 0.0, 1e30)
        aux[OWN, PEN_ROW + i : PEN_ROW + i + 1, :] = line
    aux_copy(NEAR).start()

    @pl.when(has_across)
    def _():
        aux_copy(ACROSS).start()

    loop(EARLY, chunks, start_queries)

    @pl.when(jnp.logical_not(has_across))
    def _():
        qs[ACROSS] = jnp.zeros((tile, full), LOW)
        gs[ACROSS] = jnp.zeros((tile, full), LOW)
        aux[ACROSS] = jnp.zeros((AUX_ROWS, tile), F32)

    for copy in local[2:]:
        copy.wait()
    aux_copy(NEAR).wait_recv()

    @pl.when(has_across)
    def _():
        aux_copy(ACROSS).wait_recv()

    def pick(table, index):
        chosen = lax.broadcasted_iota(jnp.int32, table.shape, 0) == index
        return jnp.sum(jnp.where(chosen, table, 0.0), 0, keepdims=True)

    def pair_block(h, slot, sources, fresh=False):
        at = head_cols(h)
        first, count = sources[0], len(sources)
        q = qs[first : first + count, :, at].reshape(count * tile, width)
        g = gs[first : first + count, :, at].reshape(count * tile, width)
        k, v = ks[slot, :, at], vs[slot, :, at]
        lines, deltas = [], []
        for source in sources:
            query_frame, row_offset = query_frames[source]
            table = aux[source]
            pen = PEN_ROW + 3 * (key_frames[slot] - query_frame + 1) + row_offset + 1
            lines.append(pick(table, h) + pick(table, pen))
            deltas.append(pick(table, DELTA_ROW + h))
        line, delta = jnp.concatenate(lines, 1), jnp.concatenate(deltas, 1)
        weights = jnp.exp2(dot(k, q, NT) * (scale * LOG2E) - line)
        grad_score = (weights * (dot(v, g, NT) - delta)).astype(LOW)
        span = slice(first * tile, (first + count) * tile)
        more = dot(k, grad_score, TN)
        dq_sum[:, span] = more if fresh else dq_sum[:, span] + more
        return dot(grad_score, q, NN) * scale, dot(weights.astype(LOW), g, NN)

    ALL, PAIR, LAST = (OWN, NEAR, ACROSS), (OWN, NEAR), (ACROSS,)

    def either(condition, body, yes, no):
        @pl.when(condition)
        def _():
            body(yes)

        @pl.when(jnp.logical_not(condition))
        def _():
            body(no)

    def finish_queries(h):
        at = head_cols(h)
        for source in (OWN, NEAR, ACROSS):
            part = dq_sum[:, source * tile : (source + 1) * tile].T * scale
            if source == OWN:
                dq_own[:, at] = part
            else:
                dq_send[source - 1, :, at] = part.astype(LOW)

    def start_dq(c):
        dq_copy(NEAR, c).start()

        @pl.when(has_across)
        def _():
            dq_copy(ACROSS, c).start()

    def send_link_grads(c):
        relayed = jnp.logical_and(outer, c < VIA_GRADS)

        @pl.when(relayed)
        def _():
            for copy in via_copies(1, c):
                copy.start()

        @pl.when(jnp.logical_not(relayed))
        def _():
            for copy in dkv_copies(LINK, to_link, c):
                copy.start()

    def merge(c):
        at = head_cols(c)
        for copy in dkv_copies(FAR, to_chip, c):
            copy.wait_recv()
        for i, (recv, send) in enumerate(((dk_recv, dk_send), (dv_recv, dv_send))):
            total = held[lax.rem(c, 2), i] + recv[FAR - 1, :, at].astype(F32)
            send[LINK - 1, :, at] = total.astype(LOW)
        send_link_grads(c)

    def compute(h):
        at = head_cols(h)
        for copy in query_copies(NEAR, h):
            copy.wait_recv()

        @pl.when(has_across)
        def _():
            for copy in query_copies(ACROSS, h):
                copy.wait_recv()

        @pl.when(jnp.logical_and(inner, h < VIA_KEYS))
        def _():
            carry(0, h)

        @pl.when(jnp.logical_and(jnp.logical_and(inner, has_link), h + LEAD < chunks))
        def _():
            start_link_keys(h + LEAD)

        for copy in key_copies(CHIP, to_chip, h):
            copy.wait_recv()

        @pl.when(has_link)
        def _():
            for copy in key_copies(LINK, to_link, h):
                copy.wait_recv()

        @pl.when(outer)
        def _():
            for copy in key_copies(FAR, to_chip, h):
                copy.start()

        def own_keys(sources):
            dk_own[:, at], dv_own[:, at] = pair_block(h, 0, sources, fresh=True)
            if ACROSS not in sources:
                dq_sum[:, ACROSS * tile :] = jnp.zeros((width, tile), F32)

        def chip_keys(sources):
            dk, dv = pair_block(h, CHIP, sources)
            dk_send[CHIP - 1, :, at] = dk.astype(LOW)
            dv_send[CHIP - 1, :, at] = dv.astype(LOW)

        def link_keys(sources):
            held[lax.rem(h, 2), 0], held[lax.rem(h, 2), 1] = pair_block(h, LINK, sources)

        either(jnp.logical_or(inner, middle), own_keys, ALL, PAIR)
        either(inner, chip_keys, ALL, PAIR)
        for copy in dkv_copies(CHIP, to_chip, h):
            copy.start()

        @pl.when(has_link)
        def _():
            either(middle, link_keys, ALL, LAST)

        @pl.when(jnp.logical_and(inner, has_link))
        def _():
            dk_send[LINK - 1, :, at] = held[lax.rem(h, 2), 0].astype(LOW)
            dv_send[LINK - 1, :, at] = held[lax.rem(h, 2), 1].astype(LOW)
            send_link_grads(h)

        @pl.when(outer)
        def _():
            for copy in key_copies(FAR, to_chip, h):
                copy.wait_recv()
            dk, dv = pair_block(h, FAR, LAST)
            dk_send[FAR - 1, :, at] = dk.astype(LOW)
            dv_send[FAR - 1, :, at] = dv.astype(LOW)
            for copy in dkv_copies(FAR, to_chip, h):
                copy.start()

        finish_queries(h)
        start_dq(h)

        @pl.when(jnp.logical_and(outer, h >= 1))
        def _():
            merge(h - 1)

    loop(0, chunks, compute)

    @pl.when(outer)
    def _():
        merge(chunks - 1)

    @pl.when(inner)
    def _():
        loop(0, VIA_GRADS, lambda c: carry(1, c))

    @pl.when(jnp.logical_not(has_link))
    def _():
        dk_recv[LINK - 1] = jnp.zeros((tile, full), LOW)
        dv_recv[LINK - 1] = jnp.zeros((tile, full), LOW)

    @pl.when(jnp.logical_not(has_across))
    def _():
        dq_recv[ACROSS - 1] = jnp.zeros((tile, full), LOW)

    def last_pass(c):
        at = cols(c)
        dq_copy(NEAR, c).wait_recv()

        @pl.when(has_across)
        def _():
            dq_copy(ACROSS, c).wait_recv()

        for copy in dkv_copies(CHIP, to_chip, c):
            copy.wait_recv()
        @pl.when(has_link)
        def _():
            for copy in dkv_copies(LINK, to_link, c):
                copy.wait_recv()
        for own, recv, out in ((dq_own, dq_recv, dq_out), (dk_own, dk_recv, dk_out), (dv_own, dv_recv, dv_out)):
            out[:, at] = (own[:, at] + recv[0, :, at].astype(F32) + recv[1, :, at].astype(F32)).astype(LOW)

    loop(0, chunks, last_pass)

    aux_copy(NEAR).wait_send()

    @pl.when(has_across)
    def _():
        aux_copy(ACROSS).wait_send()

    def drain(c):
        for copy in (*query_copies(NEAR, c), dq_copy(NEAR, c)):
            copy.wait_send()

        @pl.when(has_across)
        def _():
            for copy in (*query_copies(ACROSS, c), dq_copy(ACROSS, c)):
                copy.wait_send()

        for copy in (*key_copies(CHIP, to_chip, c), *dkv_copies(CHIP, to_chip, c)):
            copy.wait_send()
        @pl.when(has_link)
        def _():
            for copy in (*key_copies(LINK, to_link, c), *dkv_copies(LINK, to_link, c)):
                copy.wait_send()
        @pl.when(outer)
        def _():
            for copy in (*key_copies(FAR, to_chip, c), *dkv_copies(FAR, to_chip, c)):
                copy.wait_send()

    loop(0, chunks, drain)

    def drain_carried(kind):
        def run(c):
            for copy in onward_copies(kind, c):
                copy.wait_send()

        return run

    @pl.when(inner)
    def _():
        loop(0, VIA_KEYS, drain_carried(0))
        loop(0, VIA_GRADS, drain_carried(1))


def per_device(queries, keys, values, outputs, out_grads, log_sums, window_mask):
    shape = queries.shape
    tile, full = shape[2:]
    heads = log_sums.shape[2]
    width = full // heads
    chunks = heads
    flat = (tile, full)
    any_spec = pl.BlockSpec(memory_space=pl.ANY)
    vmem = pl.BlockSpec(memory_space=pltpu.VMEM)
    dma = pltpu.SemaphoreType.DMA
    grads = pl.pallas_call(
        kernel,
        out_shape=(jax.ShapeDtypeStruct(flat, LOW),) * 3,
        in_specs=[any_spec] * 5 + [vmem, pl.BlockSpec(memory_space=pltpu.SMEM)],
        out_specs=(vmem,) * 3,
        scratch_shapes=[
            *[pltpu.VMEM((3,) + flat, LOW)] * 2,
            *[pltpu.VMEM((4,) + flat, LOW)] * 2,
            pltpu.VMEM(flat, LOW),
            pltpu.VMEM((3, AUX_ROWS, tile), F32),
            pltpu.VMEM((width, 3 * tile), F32),
            pltpu.VMEM((2, 2, tile, width), F32),
            *[pltpu.VMEM(flat, F32)] * 3,
            pltpu.VMEM((2,) + flat, LOW), *[pltpu.VMEM((3,) + flat, LOW)] * 2,
            pltpu.VMEM((2,) + flat, LOW), *[pltpu.VMEM((3,) + flat, LOW)] * 2,
            pltpu.VMEM((2, 2, tile, max(VIA_KEYS, VIA_GRADS) * width), LOW),
            dma((5,)), dma((2, 2, chunks)), dma((2, 2, chunks)),
            dma((2, 2, chunks)), dma((2, 2, chunks)),
            dma((3, 2, chunks)), dma((3, 2, chunks)),
            dma((2,)), dma((2,)),
            dma((2, chunks)), dma((2, chunks)),
            dma((3, 2, chunks)), dma((3, 2, chunks)),
        ],
        compiler_params=pltpu.CompilerParams(
            collective_id=0, has_side_effects=True, vmem_limit_bytes=54 * 2**20
        ),
        name="tile_attention_backward",
    )(
        *[x.reshape(flat) for x in (queries, keys, values, outputs, out_grads)],
        log_sums.reshape(heads, 1, tile),
        window_mask.reshape(1, -1),
    )
    return tuple(g.reshape(shape) for g in grads)


def solution(mesh):
    tiles = P("tm", "space", None, None)
    return jax.shard_map(
        per_device,
        mesh=mesh,
        in_specs=(tiles,) * 6 + (P("tm", "space", None),),
        out_specs=(tiles,) * 3,
        check_vma=False,
    )
```

```python
import functools
import math

import jax
import jax.numpy as jnp
from jax import lax
from jax.experimental import pallas as pl
from jax.experimental.pallas import tpu as pltpu
from jax.sharding import PartitionSpec as P

F32 = jnp.float32
LOW = jnp.bfloat16
MESH = pl.DeviceIdType.MESH
EARLY = 2
LOG2E = math.log2(math.e)
NT = (((1,), (1,)), ((), ()))
NN = (((1,), (0,)), ((), ()))
TN = (((0,), (0,)), ((), ()))
OWN, NEAR, ACROSS = 0, 1, 2
CHIP, LINK, FAR = 1, 2, 3
DELTA_ROW, PEN_ROW, AUX_ROWS = 12, 24, 40
VIA_KEYS = 2
VIA_GRADS = 0
LEAD = 3


def dot(a, b, dims):
    return lax.dot_general(a, b, dims, preferred_element_type=F32)


def kernel(
    q_in, k_in, v_in, o_in, g_in, lse_ref, mask_ref,
    dq_out, dk_out, dv_out,
    qs, gs, ks, vs, aux, now, pens, across_sum, held, dq_own, dk_own, dv_own,
    dq_send, dk_send, dv_send, dq_recv, dk_recv, dv_recv, passing,
    in_sem, out_sem, pass_rs, pass_ss, q_ss, q_rs, kv_ss, kv_rs, aux_ss, aux_rs, dq_ss, dq_rs, dkv_ss, dkv_rs,
):
    tile, full = q_in.shape
    heads = lse_ref.shape[0]
    width = full // heads
    wide, chunks = width, heads
    scale = width**-0.5
    frame, row = lax.axis_index("tm"), lax.axis_index("space")
    frames, rows = lax.axis_size("tm"), lax.axis_size("space")
    odd = lax.rem(frame, 2)
    step = 1 - 2 * odd
    place = lax.rem(row, 4)
    toward = 1 - 2 * lax.rem(place, 2)
    partner, beyond = row + toward, row - toward
    outer = jnp.logical_or(place == 0, place == 3)
    inner = jnp.logical_not(outer)
    other = frames - 1 - frame
    middle = jnp.abs(other - frame) == 1
    has_link = jnp.logical_or(outer, middle)
    has_across = jnp.logical_and(beyond >= 0, beyond < rows)
    across_frame = jnp.where(outer, other, frame)
    to_near, to_across = (frame, partner), (across_frame, beyond)
    to_chip, to_link, to_cross = (frame + step, row), (other, row), (other, partner)
    key_frames = (frame, frame + step, other, frames - 1 - (frame + step))
    query_frames = ((frame, 0), (frame, -toward), (across_frame, toward))

    def cols(c):
        return pl.ds(pl.multiple_of(c * wide, wide), wide)

    def head_cols(h):
        return pl.ds(pl.multiple_of(h * width, width), width)

    outs = dq_send.at[0]
    local = [
        pltpu.make_async_copy(src, dst, in_sem.at[i])
        for i, (src, dst) in enumerate(
            ((o_in, outs), (g_in, gs.at[OWN]), (q_in, qs.at[OWN]), (k_in, ks.at[0]), (v_in, vs.at[0]))
        )
    ]
    for copy in local:
        copy.start()

    barrier = pltpu.get_barrier_semaphore()
    pl.semaphore_signal(barrier, inc=1, device_id=to_chip, device_id_type=MESH)
    pl.semaphore_signal(barrier, inc=1, device_id=to_near, device_id_type=MESH)
    for there, dst in ((has_across, to_across), (has_link, to_link)):
        @pl.when(there)
        def _():
            pl.semaphore_signal(barrier, inc=1, device_id=dst, device_id_type=MESH)
    pl.semaphore_signal(barrier, inc=1, device_id=to_cross, device_id_type=MESH)
    peers = 3 + has_across.astype(jnp.int32) + has_link.astype(jnp.int32)
    pl.semaphore_wait(barrier, peers)

    def remote(src, dst, ss, rs, target):
        return pltpu.make_async_remote_copy(
            src_ref=src, dst_ref=dst, send_sem=ss, recv_sem=rs,
            device_id=target, device_id_type=MESH,
        )

    def query_copies(slot, c):
        target = to_near if slot == NEAR else to_across
        return [
            remote(src.at[:, cols(c)], dst.at[slot, :, cols(c)], q_ss.at[slot - 1, i, c], q_rs.at[slot - 1, i, c], target)
            for i, (src, dst) in enumerate(((q_in, qs), (g_in, gs)))
        ]

    def aux_copy(slot):
        target = to_near if slot == NEAR else to_across
        return remote(aux.at[OWN], aux.at[slot], aux_ss.at[slot - 1], aux_rs.at[slot - 1], target)

    def key_copies(slot, target, c):
        sources = (ks.at[LINK], vs.at[LINK]) if slot == FAR else (k_in, v_in)
        return [
            remote(src.at[:, cols(c)], dst.at[slot, :, cols(c)], kv_ss.at[slot - 1, i, c], kv_rs.at[slot - 1, i, c], target)
            for i, (src, dst) in enumerate(zip(sources, (ks, vs)))
        ]

    def dq_copy(slot, c):
        target = to_near if slot == NEAR else to_across
        return remote(
            dq_send.at[slot - 1, :, cols(c)], dq_recv.at[slot - 1, :, cols(c)],
            dq_ss.at[slot - 1, c], dq_rs.at[slot - 1, c], target,
        )

    def dkv_copies(slot, target, c):
        return (
            remote(dk_send.at[slot - 1, :, cols(c)], dk_recv.at[slot - 1, :, cols(c)], dkv_ss.at[slot - 1, 0, c], dkv_rs.at[slot - 1, 0, c], target),
            remote(dv_send.at[slot - 1, :, cols(c)], dv_recv.at[slot - 1, :, cols(c)], dkv_ss.at[slot - 1, 1, c], dkv_rs.at[slot - 1, 1, c], target),
        )

    def via_copies(kind, c):
        sources, ss = (((k_in, v_in), kv_ss), ((dk_send.at[LINK - 1], dv_send.at[LINK - 1]), dkv_ss))[kind]
        return [
            remote(src.at[:, cols(c)], passing.at[kind, i, :, cols(c)], ss.at[LINK - 1, i, c], pass_rs.at[kind, i, c], to_near)
            for i, src in enumerate(sources)
        ]

    def onward_copies(kind, c):
        targets, rs = (((ks.at[LINK], vs.at[LINK]), kv_rs), ((dk_recv.at[LINK - 1], dv_recv.at[LINK - 1]), dkv_rs))[kind]
        return [
            remote(passing.at[kind, i, :, cols(c)], dst.at[:, cols(c)], pass_ss.at[kind, i, c], rs.at[LINK - 1, i, c], to_cross)
            for i, dst in enumerate(targets)
        ]

    def carry(kind, c):
        for copy in via_copies(kind, c):
            copy.wait_recv()
        for copy in onward_copies(kind, c):
            copy.start()

    def loop(first, last, body):
        def run(c, carry):
            body(c)
            return carry

        lax.fori_loop(first, last, run, 0)

    def start_queries(c):
        @pl.when(jnp.logical_and(outer, c < VIA_KEYS))
        def _():
            for copy in via_copies(0, c):
                copy.start()
        for copy in query_copies(NEAR, c):
            copy.start()

        @pl.when(has_across)
        def _():
            for copy in query_copies(ACROSS, c):
                copy.start()

    def start_keys(c):
        for copy in key_copies(CHIP, to_chip, c):
            copy.start()

    def start_link_keys(c):
        for copy in key_copies(LINK, to_link, c):
            copy.start()

    loop(0, EARLY, start_queries)
    loop(0, chunks, start_keys)

    @pl.when(jnp.logical_and(inner, has_link))
    def _():
        loop(0, LEAD, start_link_keys)

    @pl.when(outer)
    def _():
        loop(VIA_KEYS, chunks, start_link_keys)

    local[0].wait()
    local[1].wait()
    aux[OWN] = jnp.zeros((AUX_ROWS, tile), F32)
    for h in range(heads):
        aux[OWN, h : h + 1, :] = lse_ref[h] * LOG2E
    ones = jnp.ones((8, width), LOW)

    def delta_row(h):
        products = gs[OWN, :, head_cols(h)].astype(F32) * outs[:, head_cols(h)].astype(F32)
        high = products.astype(LOW)
        low = (products - high.astype(F32)).astype(LOW)
        aux[OWN, pl.ds(DELTA_ROW + h, 1), :] = (dot(ones, high, NT) + dot(ones, low, NT))[0:1]

    loop(0, heads, delta_row)
    for i in range(9):
        if i == 4:
            line = jnp.zeros((1, tile), F32)
        else:
            line = jnp.where(jnp.full((1, tile), mask_ref[0, i], jnp.int32) > 0, 0.0, 1e30)
        aux[OWN, PEN_ROW + i : PEN_ROW + i + 1, :] = line
    aux_copy(NEAR).start()

    @pl.when(has_across)
    def _():
        aux_copy(ACROSS).start()

    loop(EARLY, chunks, start_queries)

    @pl.when(jnp.logical_not(has_across))
    def _():
        qs[ACROSS] = jnp.zeros((tile, full), LOW)
        gs[ACROSS] = jnp.zeros((tile, full), LOW)
        aux[ACROSS] = jnp.zeros((AUX_ROWS, tile), F32)

    for copy in local[2:]:
        copy.wait()
    aux_copy(NEAR).wait_recv()

    @pl.when(has_across)
    def _():
        aux_copy(ACROSS).wait_recv()

    for slot in (0, CHIP, LINK, FAR):
        for source, (query_frame, row_offset) in enumerate(query_frames):
            offset = jnp.clip(key_frames[slot] - query_frame, -1, 1)
            table = aux[source, PEN_ROW : PEN_ROW + 16, :]
            chosen = lax.broadcasted_iota(jnp.int32, table.shape, 0) == 3 * (offset + 1) + row_offset + 1
            line = jnp.sum(jnp.where(chosen, table, 0.0), 0, keepdims=True)
            pens[slot : slot + 1, source * tile : (source + 1) * tile] = line

    def pick(table, index):
        chosen = lax.broadcasted_iota(jnp.int32, table.shape, 0) == index
        return jnp.sum(jnp.where(chosen, table, 0.0), 0, keepdims=True)

    def pair_block(h, slot, sources):
        at = head_cols(h)
        first, count = sources[0], len(sources)
        span = slice(first * tile, (first + count) * tile)
        q = qs[first : first + count, :, at].reshape(count * tile, width)
        g = gs[first : first + count, :, at].reshape(count * tile, width)
        k, v = ks[slot, :, at], vs[slot, :, at]
        line = now[0:1, span] + pens[slot : slot + 1, span]
        weights = jnp.exp2(dot(k, q, NT) * (scale * LOG2E) - line)
        grad_score = (weights * (dot(v, g, NT) - now[1:2, span])).astype(LOW)
        dk = dot(grad_score, q, NN) * scale
        dv = dot(weights.astype(LOW), g, NN)
        return dk, dv, dot(k, grad_score, TN)

    ALL, PAIR, LAST = (OWN, NEAR, ACROSS), (OWN, NEAR), (ACROSS,)

    def finish_queries(h, source, total):
        part = total.T * scale
        if source == OWN:
            dq_own[:, head_cols(h)] = part
        else:
            dq_send[source - 1, :, head_cols(h)] = part.astype(LOW)

    def role(h, blocks, is_outer):
        at = head_cols(h)
        totals = {}
        for slot, sources in blocks:
            dk, dv, more = pair_block(h, slot, sources)
            for i, source in enumerate(sources):
                piece = more[:, i * tile : (i + 1) * tile]
                totals[source] = totals[source] + piece if source in totals else piece
            if slot == 0:
                dk_own[:, at], dv_own[:, at] = dk, dv
            elif slot == LINK and is_outer:
                held[lax.rem(h, 2), 0], held[lax.rem(h, 2), 1] = dk, dv
            else:
                dk_send[slot - 1, :, at] = dk.astype(LOW)
                dv_send[slot - 1, :, at] = dv.astype(LOW)
        for source, total in totals.items():
            if source == ACROSS and is_outer:
                across_sum[...] = total
            else:
                finish_queries(h, source, total)

    def send_link_grads(c):
        relayed = jnp.logical_and(outer, c < VIA_GRADS)

        @pl.when(relayed)
        def _():
            for copy in via_copies(1, c):
                copy.start()

        @pl.when(jnp.logical_not(relayed))
        def _():
            for copy in dkv_copies(LINK, to_link, c):
                copy.start()

    def merge(c):
        at = head_cols(c)
        for copy in dkv_copies(FAR, to_chip, c):
            copy.wait_recv()
        for i, (recv, send) in enumerate(((dk_recv, dk_send), (dv_recv, dv_send))):
            total = held[lax.rem(c, 2), i] + recv[FAR - 1, :, at].astype(F32)
            send[LINK - 1, :, at] = total.astype(LOW)
        send_link_grads(c)

    def compute(h):
        at = head_cols(h)
        for copy in query_copies(NEAR, h):
            copy.wait_recv()

        @pl.when(has_across)
        def _():
            for copy in query_copies(ACROSS, h):
                copy.wait_recv()

        @pl.when(jnp.logical_and(inner, h < VIA_KEYS))
        def _():
            carry(0, h)

        @pl.when(jnp.logical_and(jnp.logical_and(inner, has_link), h + LEAD < chunks))
        def _():
            start_link_keys(h + LEAD)

        for copy in key_copies(CHIP, to_chip, h):
            copy.wait_recv()

        @pl.when(has_link)
        def _():
            for copy in key_copies(LINK, to_link, h):
                copy.wait_recv()

        @pl.when(outer)
        def _():
            for copy in key_copies(FAR, to_chip, h):
                copy.start()

        for source in (OWN, NEAR, ACROSS):
            span = slice(source * tile, (source + 1) * tile)
            table = aux[source]
            now[0:1, span] = pick(table, h)
            now[1:2, span] = pick(table, DELTA_ROW + h)

        for here, blocks, is_outer in (
            (jnp.logical_and(outer, middle), ((0, ALL), (CHIP, PAIR), (LINK, ALL)), True),
            (jnp.logical_and(outer, jnp.logical_not(middle)), ((0, PAIR), (CHIP, PAIR), (LINK, LAST)), True),
            (jnp.logical_and(inner, middle), ((0, ALL), (CHIP, ALL), (LINK, ALL)), False),
            (jnp.logical_and(inner, jnp.logical_not(middle)), ((0, ALL), (CHIP, ALL)), False),
        ):
            @pl.when(here)
            def _():
                role(h, blocks, is_outer)

        for copy in dkv_copies(CHIP, to_chip, h):
            copy.start()
        dq_copy(NEAR, h).start()

        @pl.when(jnp.logical_and(inner, has_link))
        def _():
            send_link_grads(h)

        @pl.when(outer)
        def _():
            for copy in key_copies(FAR, to_chip, h):
                copy.wait_recv()
            dk, dv, more = pair_block(h, FAR, LAST)
            dk_send[FAR - 1, :, at] = dk.astype(LOW)
            dv_send[FAR - 1, :, at] = dv.astype(LOW)
            finish_queries(h, ACROSS, across_sum[...] + more)
            for copy in dkv_copies(FAR, to_chip, h):
                copy.start()

        @pl.when(has_across)
        def _():
            dq_copy(ACROSS, h).start()

        @pl.when(jnp.logical_and(outer, h >= 1))
        def _():
            merge(h - 1)

    loop(0, chunks, compute)

    @pl.when(outer)
    def _():
        merge(chunks - 1)

    @pl.when(inner)
    def _():
        loop(0, VIA_GRADS, lambda c: carry(1, c))

    @pl.when(jnp.logical_not(has_link))
    def _():
        dk_recv[LINK - 1] = jnp.zeros((tile, full), LOW)
        dv_recv[LINK - 1] = jnp.zeros((tile, full), LOW)

    @pl.when(jnp.logical_not(has_across))
    def _():
        dq_recv[ACROSS - 1] = jnp.zeros((tile, full), LOW)

    results = ((dq_own, dq_recv, qs.at[OWN]), (dk_own, dk_recv, ks.at[0]), (dv_own, dv_recv, vs.at[0]))

    def out_copy(i, c):
        out = (dq_out, dk_out, dv_out)[i]
        return pltpu.make_async_copy(results[i][2].at[:, cols(c)], out.at[:, cols(c)], out_sem.at[i, c])

    def last_pass(c):
        at = cols(c)
        dq_copy(NEAR, c).wait_recv()

        @pl.when(has_across)
        def _():
            dq_copy(ACROSS, c).wait_recv()

        for copy in dkv_copies(CHIP, to_chip, c):
            copy.wait_recv()
        @pl.when(has_link)
        def _():
            for copy in dkv_copies(LINK, to_link, c):
                copy.wait_recv()
        for i, (own, recv, stage) in enumerate(results):
            stage[:, at] = (own[:, at] + recv[0, :, at].astype(F32) + recv[1, :, at].astype(F32)).astype(LOW)
            out_copy(i, c).start()

    loop(0, chunks, last_pass)

    aux_copy(NEAR).wait_send()

    @pl.when(has_across)
    def _():
        aux_copy(ACROSS).wait_send()

    def drain(c):
        for i in range(3):
            out_copy(i, c).wait()
        for copy in (*query_copies(NEAR, c), dq_copy(NEAR, c)):
            copy.wait_send()

        @pl.when(has_across)
        def _():
            for copy in (*query_copies(ACROSS, c), dq_copy(ACROSS, c)):
                copy.wait_send()

        for copy in (*key_copies(CHIP, to_chip, c), *dkv_copies(CHIP, to_chip, c)):
            copy.wait_send()
        @pl.when(has_link)
        def _():
            for copy in (*key_copies(LINK, to_link, c), *dkv_copies(LINK, to_link, c)):
                copy.wait_send()
        @pl.when(outer)
        def _():
            for copy in (*key_copies(FAR, to_chip, c), *dkv_copies(FAR, to_chip, c)):
                copy.wait_send()

    loop(0, chunks, drain)

    def drain_carried(kind):
        def run(c):
            for copy in onward_copies(kind, c):
                copy.wait_send()

        return run

    @pl.when(inner)
    def _():
        loop(0, VIA_KEYS, drain_carried(0))
        loop(0, VIA_GRADS, drain_carried(1))


def per_device(queries, keys, values, outputs, out_grads, log_sums, window_mask):
    shape = queries.shape
    tile, full = shape[2:]
    heads = log_sums.shape[2]
    width = full // heads
    chunks = heads
    flat = (tile, full)
    any_spec = pl.BlockSpec(memory_space=pl.ANY)
    vmem = pl.BlockSpec(memory_space=pltpu.VMEM)
    dma = pltpu.SemaphoreType.DMA
    grads = pl.pallas_call(
        kernel,
        out_shape=(jax.ShapeDtypeStruct(flat, LOW),) * 3,
        in_specs=[pl.BlockSpec(memory_space=pltpu.HBM)] * 5 + [vmem, pl.BlockSpec(memory_space=pltpu.SMEM)],
        out_specs=(any_spec,) * 3,
        scratch_shapes=[
            *[pltpu.VMEM((3,) + flat, LOW)] * 2,
            *[pltpu.VMEM((4,) + flat, LOW)] * 2,
            pltpu.VMEM((3, AUX_ROWS, tile), F32),
            pltpu.VMEM((8, 3 * tile), F32),
            pltpu.VMEM((8, 3 * tile), F32),
            pltpu.VMEM((width, tile), F32),
            pltpu.VMEM((2, 2, tile, width), F32),
            *[pltpu.VMEM(flat, F32)] * 3,
            pltpu.VMEM((2,) + flat, LOW), *[pltpu.VMEM((3,) + flat, LOW)] * 2,
            pltpu.VMEM((2,) + flat, LOW), *[pltpu.VMEM((3,) + flat, LOW)] * 2,
            pltpu.VMEM((2, 2, tile, max(VIA_KEYS, VIA_GRADS) * width), LOW),
            dma((5,)), dma((3, chunks)), dma((2, 2, chunks)), dma((2, 2, chunks)),
            dma((2, 2, chunks)), dma((2, 2, chunks)),
            dma((3, 2, chunks)), dma((3, 2, chunks)),
            dma((2,)), dma((2,)),
            dma((2, chunks)), dma((2, chunks)),
            dma((3, 2, chunks)), dma((3, 2, chunks)),
        ],
        compiler_params=pltpu.CompilerParams(
            collective_id=0, has_side_effects=True, vmem_limit_bytes=50 * 2**20
        ),
        name="tile_attention_backward",
    )(
        *[x.reshape(flat) for x in (queries, keys, values, outputs, out_grads)],
        log_sums.reshape(heads, 1, tile),
        window_mask.reshape(1, -1),
    )
    return tuple(g.reshape(shape) for g in grads)


def solution(mesh):
    tiles = P("tm", "space", None, None)
    return jax.shard_map(
        per_device,
        mesh=mesh,
        in_specs=(tiles,) * 6 + (P("tm", "space", None),),
        out_specs=(tiles,) * 3,
        check_vma=False,
    )
```

```python
import functools
import math

import jax
import jax.numpy as jnp
from jax import lax
from jax.experimental import pallas as pl
from jax.experimental.pallas import tpu as pltpu
from jax.sharding import PartitionSpec as P

F32 = jnp.float32
LOW = jnp.bfloat16
MESH = pl.DeviceIdType.MESH
EARLY = 2
LOG2E = math.log2(math.e)
NT = (((1,), (1,)), ((), ()))
NN = (((1,), (0,)), ((), ()))
TN = (((0,), (0,)), ((), ()))
OWN, NEAR, ACROSS = 0, 1, 2
CHIP, LINK, FAR = 1, 2, 3
DELTA_ROW, PEN_ROW, AUX_ROWS = 12, 24, 40
VIA_FIRST, VIA_LAST = 8, 11
LEAD = 3


def dot(a, b, dims):
    return lax.dot_general(a, b, dims, preferred_element_type=F32)


def kernel(
    q_in, k_in, v_in, o_in, g_in, lse_ref, mask_ref,
    dq_out, dk_out, dv_out,
    qs, gs, ks, vs, aux, now, pens, across_sum, held, dq_own, dk_own, dv_own,
    dq_send, dk_send, dv_send, dq_recv, dk_recv, dv_recv, passing,
    in_sem, out_sem, pass_rs, pass_ss, q_ss, q_rs, kv_ss, kv_rs, aux_ss, aux_rs, dq_ss, dq_rs, dkv_ss, dkv_rs,
):
    tile, full = q_in.shape
    heads = lse_ref.shape[0]
    width = full // heads
    wide, chunks = width, heads
    scale = width**-0.5
    frame, row = lax.axis_index("tm"), lax.axis_index("space")
    frames, rows = lax.axis_size("tm"), lax.axis_size("space")
    odd = lax.rem(frame, 2)
    step = 1 - 2 * odd
    place = lax.rem(row, 4)
    toward = 1 - 2 * lax.rem(place, 2)
    partner, beyond = row + toward, row - toward
    outer = jnp.logical_or(place == 0, place == 3)
    inner = jnp.logical_not(outer)
    other = frames - 1 - frame
    middle = jnp.abs(other - frame) == 1
    has_link = jnp.logical_or(outer, middle)
    has_across = jnp.logical_and(beyond >= 0, beyond < rows)
    across_frame = jnp.where(outer, other, frame)
    to_near, to_across = (frame, partner), (across_frame, beyond)
    to_chip, to_link, to_cross = (frame + step, row), (other, row), (other, partner)
    key_frames = (frame, frame + step, other, frames - 1 - (frame + step))
    query_frames = ((frame, 0), (frame, -toward), (across_frame, toward))

    def cols(c):
        return pl.ds(pl.multiple_of(c * wide, wide), wide)

    def head_cols(h):
        return pl.ds(pl.multiple_of(h * width, width), width)

    outs = dq_send.at[0]
    local = [
        pltpu.make_async_copy(src, dst, in_sem.at[i])
        for i, (src, dst) in enumerate(
            ((o_in, outs), (g_in, gs.at[OWN]), (q_in, qs.at[OWN]), (k_in, ks.at[0]), (v_in, vs.at[0]))
        )
    ]
    for copy in local:
        copy.start()

    barrier = pltpu.get_barrier_semaphore()
    pl.semaphore_signal(barrier, inc=1, device_id=to_chip, device_id_type=MESH)
    pl.semaphore_signal(barrier, inc=1, device_id=to_near, device_id_type=MESH)
    for there, dst in ((has_across, to_across), (has_link, to_link)):
        @pl.when(there)
        def _():
            pl.semaphore_signal(barrier, inc=1, device_id=dst, device_id_type=MESH)
    pl.semaphore_signal(barrier, inc=1, device_id=to_cross, device_id_type=MESH)
    peers = 3 + has_across.astype(jnp.int32) + has_link.astype(jnp.int32)
    pl.semaphore_wait(barrier, peers)

    def remote(src, dst, ss, rs, target):
        return pltpu.make_async_remote_copy(
            src_ref=src, dst_ref=dst, send_sem=ss, recv_sem=rs,
            device_id=target, device_id_type=MESH,
        )

    def query_copies(slot, c):
        target = to_near if slot == NEAR else to_across
        return [
            remote(src.at[:, cols(c)], dst.at[slot, :, cols(c)], q_ss.at[slot - 1, i, c], q_rs.at[slot - 1, i, c], target)
            for i, (src, dst) in enumerate(((q_in, qs), (g_in, gs)))
        ]

    def aux_copy(slot):
        target = to_near if slot == NEAR else to_across
        return remote(aux.at[OWN], aux.at[slot], aux_ss.at[slot - 1], aux_rs.at[slot - 1], target)

    def key_copies(slot, target, c):
        sources = (ks.at[LINK], vs.at[LINK]) if slot == FAR else (k_in, v_in)
        return [
            remote(src.at[:, cols(c)], dst.at[slot, :, cols(c)], kv_ss.at[slot - 1, i, c], kv_rs.at[slot - 1, i, c], target)
            for i, (src, dst) in enumerate(zip(sources, (ks, vs)))
        ]

    def dq_copy(slot, c):
        target = to_near if slot == NEAR else to_across
        return remote(
            dq_send.at[slot - 1, :, cols(c)], dq_recv.at[slot - 1, :, cols(c)],
            dq_ss.at[slot - 1, c], dq_rs.at[slot - 1, c], target,
        )

    def dkv_copies(slot, target, c):
        return (
            remote(dk_send.at[slot - 1, :, cols(c)], dk_recv.at[slot - 1, :, cols(c)], dkv_ss.at[slot - 1, 0, c], dkv_rs.at[slot - 1, 0, c], target),
            remote(dv_send.at[slot - 1, :, cols(c)], dv_recv.at[slot - 1, :, cols(c)], dkv_ss.at[slot - 1, 1, c], dkv_rs.at[slot - 1, 1, c], target),
        )

    def is_via(c):
        return jnp.logical_and(c >= VIA_FIRST, c < VIA_LAST)

    def via_copies(c):
        return [
            remote(src.at[:, cols(c)], passing.at[i, :, cols(c - VIA_FIRST)], kv_ss.at[LINK - 1, i, c], pass_rs.at[i, c], to_near)
            for i, src in enumerate((k_in, v_in))
        ]

    def onward_copies(c):
        return [
            remote(passing.at[i, :, cols(c - VIA_FIRST)], dst.at[LINK, :, cols(c)], pass_ss.at[i, c], kv_rs.at[LINK - 1, i, c], to_cross)
            for i, dst in enumerate((ks, vs))
        ]

    def carry(c):
        for copy in via_copies(c):
            copy.wait_recv()
        for copy in onward_copies(c):
            copy.start()

    def loop(first, last, body):
        def run(c, carry):
            body(c)
            return carry

        lax.fori_loop(first, last, run, 0)

    def start_queries(c):
        @pl.when(jnp.logical_and(outer, is_via(c)))
        def _():
            for copy in via_copies(c):
                copy.start()
        for copy in query_copies(NEAR, c):
            copy.start()

        @pl.when(has_across)
        def _():
            for copy in query_copies(ACROSS, c):
                copy.start()

    def start_keys(c):
        for copy in key_copies(CHIP, to_chip, c):
            copy.start()

    def start_link_keys(c):
        for copy in key_copies(LINK, to_link, c):
            copy.start()

    loop(0, EARLY, start_queries)
    loop(0, chunks, start_keys)

    @pl.when(jnp.logical_and(inner, has_link))
    def _():
        loop(0, LEAD, start_link_keys)

    @pl.when(outer)
    def _():
        loop(0, VIA_FIRST, start_link_keys)
        loop(VIA_LAST, chunks, start_link_keys)

    local[0].wait()
    local[1].wait()
    aux[OWN] = jnp.zeros((AUX_ROWS, tile), F32)
    for h in range(heads):
        aux[OWN, h : h + 1, :] = lse_ref[h] * LOG2E
    ones = jnp.ones((8, width), LOW)

    def delta_row(h):
        products = gs[OWN, :, head_cols(h)].astype(F32) * outs[:, head_cols(h)].astype(F32)
        high = products.astype(LOW)
        low = (products - high.astype(F32)).astype(LOW)
        aux[OWN, pl.ds(DELTA_ROW + h, 1), :] = (dot(ones, high, NT) + dot(ones, low, NT))[0:1]

    loop(0, heads, delta_row)
    for i in range(9):
        if i == 4:
            line = jnp.zeros((1, tile), F32)
        else:
            line = jnp.where(jnp.full((1, tile), mask_ref[0, i], jnp.int32) > 0, 0.0, 1e30)
        aux[OWN, PEN_ROW + i : PEN_ROW + i + 1, :] = line
    aux_copy(NEAR).start()

    @pl.when(has_across)
    def _():
        aux_copy(ACROSS).start()

    loop(EARLY, chunks, start_queries)

    @pl.when(jnp.logical_not(has_across))
    def _():
        qs[ACROSS] = jnp.zeros((tile, full), LOW)
        gs[ACROSS] = jnp.zeros((tile, full), LOW)
        aux[ACROSS] = jnp.zeros((AUX_ROWS, tile), F32)

    for copy in local[2:]:
        copy.wait()
    aux_copy(NEAR).wait_recv()

    @pl.when(has_across)
    def _():
        aux_copy(ACROSS).wait_recv()

    for slot in (0, CHIP, LINK, FAR):
        for source, (query_frame, row_offset) in enumerate(query_frames):
            offset = jnp.clip(key_frames[slot] - query_frame, -1, 1)
            table = aux[source, PEN_ROW : PEN_ROW + 16, :]
            chosen = lax.broadcasted_iota(jnp.int32, table.shape, 0) == 3 * (offset + 1) + row_offset + 1
            line = jnp.sum(jnp.where(chosen, table, 0.0), 0, keepdims=True)
            pens[slot : slot + 1, source * tile : (source + 1) * tile] = line

    def pick(table, index):
        chosen = lax.broadcasted_iota(jnp.int32, table.shape, 0) == index
        return jnp.sum(jnp.where(chosen, table, 0.0), 0, keepdims=True)

    def pair_block(h, slot, sources):
        at = head_cols(h)
        first, count = sources[0], len(sources)
        span = slice(first * tile, (first + count) * tile)
        q = qs[first : first + count, :, at].reshape(count * tile, width)
        g = gs[first : first + count, :, at].reshape(count * tile, width)
        k, v = ks[slot, :, at], vs[slot, :, at]
        line = now[0:1, span] + pens[slot : slot + 1, span]
        weights = jnp.exp2(dot(k, q, NT) * (scale * LOG2E) - line)
        grad_score = (weights * (dot(v, g, NT) - now[1:2, span])).astype(LOW)
        dk = dot(grad_score, q, NN) * scale
        dv = dot(weights.astype(LOW), g, NN)
        return dk, dv, dot(k, grad_score, TN)

    ALL, PAIR, LAST = (OWN, NEAR, ACROSS), (OWN, NEAR), (ACROSS,)

    def finish_queries(h, source, total):
        part = total.T * scale
        if source == OWN:
            dq_own[:, head_cols(h)] = part
        else:
            dq_send[source - 1, :, head_cols(h)] = part.astype(LOW)

    def role(h, blocks, is_outer):
        at = head_cols(h)
        totals = {}
        for slot, sources in blocks:
            dk, dv, more = pair_block(h, slot, sources)
            for i, source in enumerate(sources):
                piece = more[:, i * tile : (i + 1) * tile]
                totals[source] = totals[source] + piece if source in totals else piece
            if slot == 0:
                dk_own[:, at], dv_own[:, at] = dk, dv
            elif slot == LINK and is_outer:
                held[lax.rem(h, 2), 0], held[lax.rem(h, 2), 1] = dk, dv
            else:
                dk_send[slot - 1, :, at] = dk.astype(LOW)
                dv_send[slot - 1, :, at] = dv.astype(LOW)
        for source, total in totals.items():
            if source == ACROSS and is_outer:
                across_sum[...] = total
            else:
                finish_queries(h, source, total)

    def send_link_grads(c):
        for copy in dkv_copies(LINK, to_link, c):
            copy.start()

    def merge(c):
        at = head_cols(c)
        for copy in dkv_copies(FAR, to_chip, c):
            copy.wait_recv()
        for i, (recv, send) in enumerate(((dk_recv, dk_send), (dv_recv, dv_send))):
            total = held[lax.rem(c, 2), i] + recv[FAR - 1, :, at].astype(F32)
            send[LINK - 1, :, at] = total.astype(LOW)
        send_link_grads(c)

    def compute(h):
        at = head_cols(h)
        for copy in query_copies(NEAR, h):
            copy.wait_recv()

        @pl.when(has_across)
        def _():
            for copy in query_copies(ACROSS, h):
                copy.wait_recv()

        @pl.when(jnp.logical_and(inner, is_via(h)))
        def _():
            carry(h)

        @pl.when(jnp.logical_and(jnp.logical_and(inner, has_link), h + LEAD < chunks))
        def _():
            start_link_keys(h + LEAD)

        for copy in key_copies(CHIP, to_chip, h):
            copy.wait_recv()

        @pl.when(has_link)
        def _():
            for copy in key_copies(LINK, to_link, h):
                copy.wait_recv()

        @pl.when(outer)
        def _():
            for copy in key_copies(FAR, to_chip, h):
                copy.start()

        for source in (OWN, NEAR, ACROSS):
            span = slice(source * tile, (source + 1) * tile)
            table = aux[source]
            now[0:1, span] = pick(table, h)
            now[1:2, span] = pick(table, DELTA_ROW + h)

        for here, blocks, is_outer in (
            (jnp.logical_and(outer, middle), ((0, ALL), (CHIP, PAIR), (LINK, ALL)), True),
            (jnp.logical_and(outer, jnp.logical_not(middle)), ((0, PAIR), (CHIP, PAIR), (LINK, LAST)), True),
            (jnp.logical_and(inner, middle), ((0, ALL), (CHIP, ALL), (LINK, ALL)), False),
            (jnp.logical_and(inner, jnp.logical_not(middle)), ((0, ALL), (CHIP, ALL)), False),
        ):
            @pl.when(here)
            def _():
                role(h, blocks, is_outer)

        for copy in dkv_copies(CHIP, to_chip, h):
            copy.start()
        dq_copy(NEAR, h).start()

        @pl.when(jnp.logical_and(inner, has_link))
        def _():
            send_link_grads(h)

        @pl.when(outer)
        def _():
            for copy in key_copies(FAR, to_chip, h):
                copy.wait_recv()
            dk, dv, more = pair_block(h, FAR, LAST)
            dk_send[FAR - 1, :, at] = dk.astype(LOW)
            dv_send[FAR - 1, :, at] = dv.astype(LOW)
            finish_queries(h, ACROSS, across_sum[...] + more)
            for copy in dkv_copies(FAR, to_chip, h):
                copy.start()

        @pl.when(has_across)
        def _():
            dq_copy(ACROSS, h).start()

        @pl.when(jnp.logical_and(outer, h >= 1))
        def _():
            merge(h - 1)

    loop(0, chunks, compute)

    @pl.when(outer)
    def _():
        merge(chunks - 1)

    @pl.when(jnp.logical_not(has_link))
    def _():
        dk_recv[LINK - 1] = jnp.zeros((tile, full), LOW)
        dv_recv[LINK - 1] = jnp.zeros((tile, full), LOW)

    @pl.when(jnp.logical_not(has_across))
    def _():
        dq_recv[ACROSS - 1] = jnp.zeros((tile, full), LOW)

    results = ((dq_own, dq_recv, qs.at[OWN]), (dk_own, dk_recv, ks.at[0]), (dv_own, dv_recv, vs.at[0]))

    def out_copy(i, c):
        out = (dq_out, dk_out, dv_out)[i]
        return pltpu.make_async_copy(results[i][2].at[:, cols(c)], out.at[:, cols(c)], out_sem.at[i, c])

    def last_pass(c):
        at = cols(c)
        dq_copy(NEAR, c).wait_recv()

        @pl.when(has_across)
        def _():
            dq_copy(ACROSS, c).wait_recv()

        for copy in dkv_copies(CHIP, to_chip, c):
            copy.wait_recv()
        @pl.when(has_link)
        def _():
            for copy in dkv_copies(LINK, to_link, c):
                copy.wait_recv()
        for i, (own, recv, stage) in enumerate(results):
            stage[:, at] = (own[:, at] + recv[0, :, at].astype(F32) + recv[1, :, at].astype(F32)).astype(LOW)
            out_copy(i, c).start()

    loop(0, chunks, last_pass)

    aux_copy(NEAR).wait_send()

    @pl.when(has_across)
    def _():
        aux_copy(ACROSS).wait_send()

    def drain(c):
        for i in range(3):
            out_copy(i, c).wait()
        for copy in (*query_copies(NEAR, c), dq_copy(NEAR, c)):
            copy.wait_send()

        @pl.when(has_across)
        def _():
            for copy in (*query_copies(ACROSS, c), dq_copy(ACROSS, c)):
                copy.wait_send()

        for copy in (*key_copies(CHIP, to_chip, c), *dkv_copies(CHIP, to_chip, c)):
            copy.wait_send()
        @pl.when(has_link)
        def _():
            for copy in (*key_copies(LINK, to_link, c), *dkv_copies(LINK, to_link, c)):
                copy.wait_send()
        @pl.when(outer)
        def _():
            for copy in (*key_copies(FAR, to_chip, c), *dkv_copies(FAR, to_chip, c)):
                copy.wait_send()

    loop(0, chunks, drain)

    def drain_carried(c):
        for copy in onward_copies(c):
            copy.wait_send()

    @pl.when(inner)
    def _():
        loop(VIA_FIRST, VIA_LAST, drain_carried)


def per_device(queries, keys, values, outputs, out_grads, log_sums, window_mask):
    shape = queries.shape
    tile, full = shape[2:]
    heads = log_sums.shape[2]
    width = full // heads
    chunks = heads
    flat = (tile, full)
    any_spec = pl.BlockSpec(memory_space=pl.ANY)
    vmem = pl.BlockSpec(memory_space=pltpu.VMEM)
    dma = pltpu.SemaphoreType.DMA
    grads = pl.pallas_call(
        kernel,
        out_shape=(jax.ShapeDtypeStruct(flat, LOW),) * 3,
        in_specs=[pl.BlockSpec(memory_space=pltpu.HBM)] * 5 + [vmem, pl.BlockSpec(memory_space=pltpu.SMEM)],
        out_specs=(any_spec,) * 3,
        scratch_shapes=[
            *[pltpu.VMEM((3,) + flat, LOW)] * 2,
            *[pltpu.VMEM((4,) + flat, LOW)] * 2,
            pltpu.VMEM((3, AUX_ROWS, tile), F32),
            pltpu.VMEM((8, 3 * tile), F32),
            pltpu.VMEM((8, 3 * tile), F32),
            pltpu.VMEM((width, tile), F32),
            pltpu.VMEM((2, 2, tile, width), F32),
            *[pltpu.VMEM(flat, F32)] * 3,
            pltpu.VMEM((2,) + flat, LOW), *[pltpu.VMEM((3,) + flat, LOW)] * 2,
            pltpu.VMEM((2,) + flat, LOW), *[pltpu.VMEM((3,) + flat, LOW)] * 2,
            pltpu.VMEM((2, tile, (VIA_LAST - VIA_FIRST) * width), LOW),
            dma((5,)), dma((3, chunks)), dma((2, chunks)), dma((2, chunks)),
            dma((2, 2, chunks)), dma((2, 2, chunks)),
            dma((3, 2, chunks)), dma((3, 2, chunks)),
            dma((2,)), dma((2,)),
            dma((2, chunks)), dma((2, chunks)),
            dma((3, 2, chunks)), dma((3, 2, chunks)),
        ],
        compiler_params=pltpu.CompilerParams(
            collective_id=0, has_side_effects=True, vmem_limit_bytes=50 * 2**20
        ),
        name="tile_attention_backward",
    )(
        *[x.reshape(flat) for x in (queries, keys, values, outputs, out_grads)],
        log_sums.reshape(heads, 1, tile),
        window_mask.reshape(1, -1),
    )
    return tuple(g.reshape(shape) for g in grads)


def solution(mesh):
    tiles = P("tm", "space", None, None)
    return jax.shard_map(
        per_device,
        mesh=mesh,
        in_specs=(tiles,) * 6 + (P("tm", "space", None),),
        out_specs=(tiles,) * 3,
        check_vma=False,
    )
```

```python
import functools
import math

import jax
import jax.numpy as jnp
from jax import lax
from jax.experimental import pallas as pl
from jax.experimental.pallas import tpu as pltpu
from jax.sharding import PartitionSpec as P

F32 = jnp.float32
LOW = jnp.bfloat16
MESH = pl.DeviceIdType.MESH
EARLY = 2
LOG2E = math.log2(math.e)
NT = (((1,), (1,)), ((), ()))
NN = (((1,), (0,)), ((), ()))
TN = (((0,), (0,)), ((), ()))
OWN, NEAR, ACROSS = 0, 1, 2
CHIP, LINK, FAR = 1, 2, 3
DELTA_ROW, PEN_ROW, AUX_ROWS = 12, 24, 40
VIA_FIRST, VIA_LAST = 8, 11
LEAD = 3


def dot(a, b, dims):
    return lax.dot_general(a, b, dims, preferred_element_type=F32)


def kernel(
    q_in, k_in, v_in, o_in, g_in, lse_ref, mask_ref,
    dq_out, dk_out, dv_out,
    qs, gs, ks, vs, aux, now, pens, across_sum, held, dq_own, dk_own, dv_own,
    dq_send, dk_send, dv_send, dq_recv, dk_recv, dv_recv, passing,
    in_sem, out_sem, pass_rs, pass_ss, q_ss, q_rs, kv_ss, kv_rs, aux_ss, aux_rs, dq_ss, dq_rs, dkv_ss, dkv_rs,
):
    tile, full = q_in.shape
    heads = lse_ref.shape[0]
    width = full // heads
    wide, chunks = width, heads
    scale = width**-0.5
    frame, row = lax.axis_index("tm"), lax.axis_index("space")
    frames, rows = lax.axis_size("tm"), lax.axis_size("space")
    odd = lax.rem(frame, 2)
    step = 1 - 2 * odd
    place = lax.rem(row, 4)
    toward = 1 - 2 * lax.rem(place, 2)
    partner, beyond = row + toward, row - toward
    outer = jnp.logical_or(place == 0, place == 3)
    inner = jnp.logical_not(outer)
    other = frames - 1 - frame
    middle = jnp.abs(other - frame) == 1
    has_link = jnp.logical_or(outer, middle)
    has_across = jnp.logical_and(beyond >= 0, beyond < rows)
    across_frame = jnp.where(outer, other, frame)
    to_near, to_across = (frame, partner), (across_frame, beyond)
    to_chip, to_link, to_cross = (frame + step, row), (other, row), (other, partner)
    key_frames = (frame, frame + step, other, frames - 1 - (frame + step))
    query_frames = ((frame, 0), (frame, -toward), (across_frame, toward))

    def cols(c):
        return pl.ds(pl.multiple_of(c * wide, wide), wide)

    def head_cols(h):
        return pl.ds(pl.multiple_of(h * width, width), width)

    outs = dq_send.at[0]
    local = [
        pltpu.make_async_copy(src, dst, in_sem.at[i])
        for i, (src, dst) in enumerate(
            ((o_in, outs), (g_in, gs.at[OWN]), (q_in, qs.at[OWN]), (k_in, ks.at[0]), (v_in, vs.at[0]))
        )
    ]
    for copy in local:
        copy.start()

    barrier = pltpu.get_barrier_semaphore()
    pl.semaphore_signal(barrier, inc=1, device_id=to_chip, device_id_type=MESH)
    pl.semaphore_signal(barrier, inc=1, device_id=to_near, device_id_type=MESH)
    for there, dst in ((has_across, to_across), (has_link, to_link)):
        @pl.when(there)
        def _():
            pl.semaphore_signal(barrier, inc=1, device_id=dst, device_id_type=MESH)
    pl.semaphore_signal(barrier, inc=1, device_id=to_cross, device_id_type=MESH)
    peers = 3 + has_across.astype(jnp.int32) + has_link.astype(jnp.int32)
    pl.semaphore_wait(barrier, peers)

    def remote(src, dst, ss, rs, target):
        return pltpu.make_async_remote_copy(
            src_ref=src, dst_ref=dst, send_sem=ss, recv_sem=rs,
            device_id=target, device_id_type=MESH,
        )

    def query_copies(slot, c):
        target = to_near if slot == NEAR else to_across
        return [
            remote(src.at[:, cols(c)], dst.at[slot, :, cols(c)], q_ss.at[slot - 1, i, c], q_rs.at[slot - 1, i, c], target)
            for i, (src, dst) in enumerate(((q_in, qs), (g_in, gs)))
        ]

    def aux_copy(slot):
        target = to_near if slot == NEAR else to_across
        return remote(aux.at[OWN], aux.at[slot], aux_ss.at[slot - 1], aux_rs.at[slot - 1], target)

    def key_copies(slot, target, c):
        sources = (ks.at[LINK], vs.at[LINK]) if slot == FAR else (k_in, v_in)
        return [
            remote(src.at[:, cols(c)], dst.at[slot, :, cols(c)], kv_ss.at[slot - 1, i, c], kv_rs.at[slot - 1, i, c], target)
            for i, (src, dst) in enumerate(zip(sources, (ks, vs)))
        ]

    def dq_copy(slot, c):
        target = to_near if slot == NEAR else to_across
        return remote(
            dq_send.at[slot - 1, :, cols(c)], dq_recv.at[slot - 1, :, cols(c)],
            dq_ss.at[slot - 1, c], dq_rs.at[slot - 1, c], target,
        )

    def dkv_copies(slot, target, c):
        return (
            remote(dk_send.at[slot - 1, :, cols(c)], dk_recv.at[slot - 1, :, cols(c)], dkv_ss.at[slot - 1, 0, c], dkv_rs.at[slot - 1, 0, c], target),
            remote(dv_send.at[slot - 1, :, cols(c)], dv_recv.at[slot - 1, :, cols(c)], dkv_ss.at[slot - 1, 1, c], dkv_rs.at[slot - 1, 1, c], target),
        )

    def is_via(c):
        return jnp.logical_and(c >= VIA_FIRST, c < VIA_LAST)

    def via_copies(c):
        return [
            remote(src.at[:, cols(c)], passing.at[i, :, cols(c - VIA_FIRST)], kv_ss.at[LINK - 1, i, c], pass_rs.at[i, c], to_near)
            for i, src in enumerate((k_in, v_in))
        ]

    def onward_copies(c):
        return [
            remote(passing.at[i, :, cols(c - VIA_FIRST)], dst.at[LINK, :, cols(c)], pass_ss.at[i, c], kv_rs.at[LINK - 1, i, c], to_cross)
            for i, dst in enumerate((ks, vs))
        ]

    def carry(c):
        for copy in via_copies(c):
            copy.wait_recv()
        for copy in onward_copies(c):
            copy.start()

    def loop(first, last, body):
        def run(c, carry):
            body(c)
            return carry

        lax.fori_loop(first, last, run, 0)

    def start_queries(c):
        @pl.when(jnp.logical_and(outer, is_via(c)))
        def _():
            for copy in via_copies(c):
                copy.start()
        for copy in query_copies(NEAR, c):
            copy.start()

        @pl.when(has_across)
        def _():
            for copy in query_copies(ACROSS, c):
                copy.start()

    def start_keys(c):
        for copy in key_copies(CHIP, to_chip, c):
            copy.start()

    def start_link_keys(c):
        for copy in key_copies(LINK, to_link, c):
            copy.start()

    loop(0, EARLY, start_queries)
    loop(0, chunks, start_keys)

    @pl.when(jnp.logical_and(inner, has_link))
    def _():
        loop(0, LEAD, start_link_keys)

    @pl.when(outer)
    def _():
        loop(0, VIA_FIRST, start_link_keys)
        loop(VIA_LAST, chunks, start_link_keys)

    local[0].wait()
    local[1].wait()
    aux[OWN] = jnp.zeros((AUX_ROWS, tile), F32)
    for h in range(heads):
        aux[OWN, h : h + 1, :] = lse_ref[h] * LOG2E
    ones = jnp.ones((8, width), LOW)

    def delta_row(h):
        products = gs[OWN, :, head_cols(h)].astype(F32) * outs[:, head_cols(h)].astype(F32)
        high = products.astype(LOW)
        low = (products - high.astype(F32)).astype(LOW)
        aux[OWN, pl.ds(DELTA_ROW + h, 1), :] = (dot(ones, high, NT) + dot(ones, low, NT))[0:1]

    loop(0, heads, delta_row)
    for i in range(9):
        if i == 4:
            line = jnp.zeros((1, tile), F32)
        else:
            line = jnp.where(jnp.full((1, tile), mask_ref[0, i], jnp.int32) > 0, 0.0, 1e30)
        aux[OWN, PEN_ROW + i : PEN_ROW + i + 1, :] = line
    aux_copy(NEAR).start()

    @pl.when(has_across)
    def _():
        aux_copy(ACROSS).start()

    loop(EARLY, chunks, start_queries)

    @pl.when(jnp.logical_not(has_across))
    def _():
        qs[ACROSS] = jnp.zeros((tile, full), LOW)
        gs[ACROSS] = jnp.zeros((tile, full), LOW)
        aux[ACROSS] = jnp.zeros((AUX_ROWS, tile), F32)

    for copy in local[2:]:
        copy.wait()
    aux_copy(NEAR).wait_recv()

    @pl.when(has_across)
    def _():
        aux_copy(ACROSS).wait_recv()

    for slot in (0, CHIP, LINK, FAR):
        for source, (query_frame, row_offset) in enumerate(query_frames):
            offset = jnp.clip(key_frames[slot] - query_frame, -1, 1)
            table = aux[source, PEN_ROW : PEN_ROW + 16, :]
            chosen = lax.broadcasted_iota(jnp.int32, table.shape, 0) == 3 * (offset + 1) + row_offset + 1
            line = jnp.sum(jnp.where(chosen, table, 0.0), 0, keepdims=True)
            pens[slot : slot + 1, source * tile : (source + 1) * tile] = line

    def pick(table, index):
        chosen = lax.broadcasted_iota(jnp.int32, table.shape, 0) == index
        return jnp.sum(jnp.where(chosen, table, 0.0), 0, keepdims=True)

    def pair_block(h, slot, sources):
        at = head_cols(h)
        first, count = sources[0], len(sources)
        span = slice(first * tile, (first + count) * tile)
        q = qs[first : first + count, :, at].reshape(count * tile, width)
        g = gs[first : first + count, :, at].reshape(count * tile, width)
        k, v = ks[slot, :, at], vs[slot, :, at]
        line = now[0:1, span] + pens[slot : slot + 1, span]
        weights = jnp.exp2(dot(k, q, NT) * (scale * LOG2E) - line)
        grad_score = (weights * (dot(v, g, NT) - now[1:2, span])).astype(LOW)
        dk = dot(grad_score, q, NN) * scale
        dv = dot(weights.astype(LOW), g, NN)
        return dk, dv, dot(k, grad_score, TN)

    ALL, PAIR, LAST = (OWN, NEAR, ACROSS), (OWN, NEAR), (ACROSS,)

    def finish_queries(h, source, total):
        part = total.T * scale
        if source == OWN:
            dq_own[:, head_cols(h)] = part
        else:
            dq_send[source - 1, :, head_cols(h)] = part.astype(LOW)

    def role(h, blocks, is_outer):
        at = head_cols(h)
        totals = {}
        for slot, sources in blocks:
            dk, dv, more = pair_block(h, slot, sources)
            for i, source in enumerate(sources):
                piece = more[:, i * tile : (i + 1) * tile]
                totals[source] = totals[source] + piece if source in totals else piece
            if slot == 0:
                dk_own[:, at], dv_own[:, at] = dk, dv
            elif slot == LINK and is_outer:
                held[lax.rem(h, 2), 0], held[lax.rem(h, 2), 1] = dk, dv
            else:
                dk_send[slot - 1, :, at] = dk.astype(LOW)
                dv_send[slot - 1, :, at] = dv.astype(LOW)
        for source, total in totals.items():
            if source == ACROSS and is_outer:
                across_sum[...] = total
            else:
                finish_queries(h, source, total)

    def send_link_grads(c):
        for copy in dkv_copies(LINK, to_link, c):
            copy.start()

    def merge(c):
        at = head_cols(c)
        for copy in dkv_copies(FAR, to_chip, c):
            copy.wait_recv()
        for i, (recv, send) in enumerate(((dk_recv, dk_send), (dv_recv, dv_send))):
            total = held[lax.rem(c, 2), i] + recv[FAR - 1, :, at].astype(F32)
            send[LINK - 1, :, at] = total.astype(LOW)
        send_link_grads(c)

    def compute(h):
        at = head_cols(h)
        for copy in query_copies(NEAR, h):
            copy.wait_recv()

        @pl.when(has_across)
        def _():
            for copy in query_copies(ACROSS, h):
                copy.wait_recv()

        @pl.when(jnp.logical_and(inner, is_via(h)))
        def _():
            carry(h)

        @pl.when(jnp.logical_and(jnp.logical_and(inner, has_link), h + LEAD < chunks))
        def _():
            start_link_keys(h + LEAD)

        for copy in key_copies(CHIP, to_chip, h):
            copy.wait_recv()

        @pl.when(has_link)
        def _():
            for copy in key_copies(LINK, to_link, h):
                copy.wait_recv()

        @pl.when(outer)
        def _():
            for copy in key_copies(FAR, to_chip, h):
                copy.start()

        for source in (OWN, NEAR, ACROSS):
            span = slice(source * tile, (source + 1) * tile)
            table = aux[source]
            now[0:1, span] = pick(table, h)
            now[1:2, span] = pick(table, DELTA_ROW + h)

        for here, blocks, is_outer in (
            (jnp.logical_and(outer, middle), ((0, ALL), (CHIP, PAIR), (LINK, ALL)), True),
            (jnp.logical_and(outer, jnp.logical_not(middle)), ((0, PAIR), (CHIP, PAIR), (LINK, LAST)), True),
            (jnp.logical_and(inner, middle), ((0, ALL), (CHIP, ALL), (LINK, ALL)), False),
            (jnp.logical_and(inner, jnp.logical_not(middle)), ((0, ALL), (CHIP, ALL)), False),
        ):
            @pl.when(here)
            def _():
                role(h, blocks, is_outer)

        for copy in dkv_copies(CHIP, to_chip, h):
            copy.start()
        dq_copy(NEAR, h).start()

        @pl.when(jnp.logical_and(inner, has_link))
        def _():
            send_link_grads(h)

        @pl.when(outer)
        def _():
            for copy in key_copies(FAR, to_chip, h):
                copy.wait_recv()
            dk, dv, more = pair_block(h, FAR, LAST)
            dk_send[FAR - 1, :, at] = dk.astype(LOW)
            dv_send[FAR - 1, :, at] = dv.astype(LOW)
            finish_queries(h, ACROSS, across_sum[...] + more)
            for copy in dkv_copies(FAR, to_chip, h):
                copy.start()

        @pl.when(has_across)
        def _():
            dq_copy(ACROSS, h).start()

        @pl.when(jnp.logical_and(outer, h >= 1))
        def _():
            merge(h - 1)

    loop(0, chunks, compute)

    @pl.when(outer)
    def _():
        merge(chunks - 1)

    @pl.when(jnp.logical_not(has_link))
    def _():
        dk_recv[LINK - 1] = jnp.zeros((tile, full), LOW)
        dv_recv[LINK - 1] = jnp.zeros((tile, full), LOW)

    @pl.when(jnp.logical_not(has_across))
    def _():
        dq_recv[ACROSS - 1] = jnp.zeros((tile, full), LOW)

    results = ((dq_own, dq_recv, qs.at[OWN]), (dk_own, dk_recv, ks.at[0]), (dv_own, dv_recv, vs.at[0]))

    def out_copy(i, c):
        out = (dq_out, dk_out, dv_out)[i]
        return pltpu.make_async_copy(results[i][2].at[:, cols(c)], out.at[:, cols(c)], out_sem.at[i, c])

    def last_pass(c):
        at = cols(c)
        dq_copy(NEAR, c).wait_recv()

        @pl.when(has_across)
        def _():
            dq_copy(ACROSS, c).wait_recv()

        for copy in dkv_copies(CHIP, to_chip, c):
            copy.wait_recv()
        @pl.when(has_link)
        def _():
            for copy in dkv_copies(LINK, to_link, c):
                copy.wait_recv()
        for i, (own, recv, stage) in enumerate(results):
            stage[:, at] = (own[:, at] + recv[0, :, at].astype(F32) + recv[1, :, at].astype(F32)).astype(LOW)
            out_copy(i, c).start()

    loop(0, chunks, last_pass)

    aux_copy(NEAR).wait_send()

    @pl.when(has_across)
    def _():
        aux_copy(ACROSS).wait_send()

    def drain(c):
        for i in range(3):
            out_copy(i, c).wait()
        for copy in (*query_copies(NEAR, c), dq_copy(NEAR, c)):
            copy.wait_send()

        @pl.when(has_across)
        def _():
            for copy in (*query_copies(ACROSS, c), dq_copy(ACROSS, c)):
                copy.wait_send()

        for copy in (*key_copies(CHIP, to_chip, c), *dkv_copies(CHIP, to_chip, c)):
            copy.wait_send()
        @pl.when(has_link)
        def _():
            for copy in (*key_copies(LINK, to_link, c), *dkv_copies(LINK, to_link, c)):
                copy.wait_send()
        @pl.when(outer)
        def _():
            for copy in (*key_copies(FAR, to_chip, c), *dkv_copies(FAR, to_chip, c)):
                copy.wait_send()

    loop(0, chunks, drain)

    def drain_carried(c):
        for copy in onward_copies(c):
            copy.wait_send()

    @pl.when(inner)
    def _():
        loop(VIA_FIRST, VIA_LAST, drain_carried)


def store_kernel(*refs):
    sources, targets, sem = refs[:3], refs[3:6], refs[6]
    copies = [pltpu.make_async_copy(a, b, sem.at[i]) for i, (a, b) in enumerate(zip(sources, targets))]
    for copy in copies:
        copy.start()
    for copy in copies:
        copy.wait()


def per_device(queries, keys, values, outputs, out_grads, log_sums, window_mask):
    shape = queries.shape
    tile, full = shape[2:]
    heads = log_sums.shape[2]
    width = full // heads
    chunks = heads
    flat = (tile, full)
    any_spec = pl.BlockSpec(memory_space=pl.ANY)
    vmem = pl.BlockSpec(memory_space=pltpu.VMEM)
    dma = pltpu.SemaphoreType.DMA
    grads = pl.pallas_call(
        kernel,
        out_shape=(jax.ShapeDtypeStruct(flat, LOW),) * 3,
        in_specs=[pl.BlockSpec(memory_space=pltpu.HBM)] * 5 + [vmem, pl.BlockSpec(memory_space=pltpu.SMEM)],
        out_specs=(any_spec,) * 3,
        scratch_shapes=[
            *[pltpu.VMEM((3,) + flat, LOW)] * 2,
            *[pltpu.VMEM((4,) + flat, LOW)] * 2,
            pltpu.VMEM((3, AUX_ROWS, tile), F32),
            pltpu.VMEM((8, 3 * tile), F32),
            pltpu.VMEM((8, 3 * tile), F32),
            pltpu.VMEM((width, tile), F32),
            pltpu.VMEM((2, 2, tile, width), F32),
            *[pltpu.VMEM(flat, F32)] * 3,
            pltpu.VMEM((2,) + flat, LOW), *[pltpu.VMEM((3,) + flat, LOW)] * 2,
            pltpu.VMEM((2,) + flat, LOW), *[pltpu.VMEM((3,) + flat, LOW)] * 2,
            pltpu.VMEM((2, tile, (VIA_LAST - VIA_FIRST) * width), LOW),
            dma((5,)), dma((3, chunks)), dma((2, chunks)), dma((2, chunks)),
            dma((2, 2, chunks)), dma((2, 2, chunks)),
            dma((3, 2, chunks)), dma((3, 2, chunks)),
            dma((2,)), dma((2,)),
            dma((2, chunks)), dma((2, chunks)),
            dma((3, 2, chunks)), dma((3, 2, chunks)),
        ],
        compiler_params=pltpu.CompilerParams(
            collective_id=0, has_side_effects=True, vmem_limit_bytes=50 * 2**20
        ),
        name="tile_attention_backward",
    )(
        *[x.reshape(flat) for x in (queries, keys, values, outputs, out_grads)],
        log_sums.reshape(heads, 1, tile),
        window_mask.reshape(1, -1),
    )
    stored = pl.pallas_call(
        store_kernel,
        out_shape=(jax.ShapeDtypeStruct(flat, LOW),) * 3,
        in_specs=[vmem] * 3,
        out_specs=(pl.BlockSpec(memory_space=pltpu.HBM),) * 3,
        scratch_shapes=[dma((3,))],
        compiler_params=pltpu.CompilerParams(vmem_limit_bytes=8 * 2**20),
        name="store_gradients",
    )(*grads)
    return tuple(g.reshape(shape) for g in stored)


def solution(mesh):
    tiles = P("tm", "space", None, None)
    return jax.shard_map(
        per_device,
        mesh=mesh,
        in_specs=(tiles,) * 6 + (P("tm", "space", None),),
        out_specs=(tiles,) * 3,
        check_vma=False,
    )
```

```python
import functools
import math

import jax
import jax.numpy as jnp
from jax import lax
from jax.experimental import pallas as pl
from jax.experimental.pallas import tpu as pltpu
from jax.sharding import PartitionSpec as P

F32 = jnp.float32
LOW = jnp.bfloat16
MESH = pl.DeviceIdType.MESH
EARLY = 2
LOG2E = math.log2(math.e)
NT = (((1,), (1,)), ((), ()))
NN = (((1,), (0,)), ((), ()))
TN = (((0,), (0,)), ((), ()))
OWN, NEAR, ACROSS = 0, 1, 2
CHIP, LINK, FAR = 1, 2, 3
DELTA_ROW, PEN_ROW, AUX_ROWS = 12, 24, 40
VIA_FIRST, VIA_LAST = 8, 11
LEAD = 3


def dot(a, b, dims):
    return lax.dot_general(a, b, dims, preferred_element_type=F32)


def kernel(
    q_in, k_in, v_in, o_in, g_in, lse_in, mask_in,
    dq_out, dk_out, dv_out,
    lse_ref, mask_ref, qs, gs, ks, vs, aux, now, pens, across_sum, held, dq_own, dk_own, dv_own,
    dq_send, dk_send, dv_send, dq_recv, dk_recv, dv_recv, passing,
    in_sem, out_sem, pass_rs, pass_ss, q_ss, q_rs, kv_ss, kv_rs, aux_ss, aux_rs, dq_ss, dq_rs, dkv_ss, dkv_rs,
):
    tile, full = q_in.shape
    heads = lse_ref.shape[0]
    width = full // heads
    wide, chunks = width, heads
    scale = width**-0.5
    frame, row = lax.axis_index("tm"), lax.axis_index("space")
    frames, rows = lax.axis_size("tm"), lax.axis_size("space")
    odd = lax.rem(frame, 2)
    step = 1 - 2 * odd
    place = lax.rem(row, 4)
    toward = 1 - 2 * lax.rem(place, 2)
    partner, beyond = row + toward, row - toward
    outer = jnp.logical_or(place == 0, place == 3)
    inner = jnp.logical_not(outer)
    other = frames - 1 - frame
    middle = jnp.abs(other - frame) == 1
    has_link = jnp.logical_or(outer, middle)
    has_across = jnp.logical_and(beyond >= 0, beyond < rows)
    across_frame = jnp.where(outer, other, frame)
    to_near, to_across = (frame, partner), (across_frame, beyond)
    to_chip, to_link, to_cross = (frame + step, row), (other, row), (other, partner)
    key_frames = (frame, frame + step, other, frames - 1 - (frame + step))
    query_frames = ((frame, 0), (frame, -toward), (across_frame, toward))

    def cols(c):
        return pl.ds(pl.multiple_of(c * wide, wide), wide)

    def head_cols(h):
        return pl.ds(pl.multiple_of(h * width, width), width)

    outs = dq_send.at[0]
    local = [
        pltpu.make_async_copy(src, dst, in_sem.at[i])
        for i, (src, dst) in enumerate(
            (
                (o_in, outs), (g_in, gs.at[OWN]), (lse_in, lse_ref), (mask_in, mask_ref),
                (q_in, qs.at[OWN]), (k_in, ks.at[0]), (v_in, vs.at[0]),
            )
        )
    ]

    barrier = pltpu.get_barrier_semaphore()
    pl.semaphore_signal(barrier, inc=1, device_id=to_chip, device_id_type=MESH)
    pl.semaphore_signal(barrier, inc=1, device_id=to_near, device_id_type=MESH)
    for there, dst in ((has_across, to_across), (has_link, to_link)):
        @pl.when(there)
        def _():
            pl.semaphore_signal(barrier, inc=1, device_id=dst, device_id_type=MESH)
    pl.semaphore_signal(barrier, inc=1, device_id=to_cross, device_id_type=MESH)
    for copy in local:
        copy.start()
    peers = 3 + has_across.astype(jnp.int32) + has_link.astype(jnp.int32)
    pl.semaphore_wait(barrier, peers)

    def remote(src, dst, ss, rs, target):
        return pltpu.make_async_remote_copy(
            src_ref=src, dst_ref=dst, send_sem=ss, recv_sem=rs,
            device_id=target, device_id_type=MESH,
        )

    def query_copies(slot, c):
        target = to_near if slot == NEAR else to_across
        return [
            remote(src.at[:, cols(c)], dst.at[slot, :, cols(c)], q_ss.at[slot - 1, i, c], q_rs.at[slot - 1, i, c], target)
            for i, (src, dst) in enumerate(((q_in, qs), (g_in, gs)))
        ]

    def aux_copy(slot):
        target = to_near if slot == NEAR else to_across
        return remote(aux.at[OWN], aux.at[slot], aux_ss.at[slot - 1], aux_rs.at[slot - 1], target)

    def key_copies(slot, target, c):
        sources = (ks.at[LINK], vs.at[LINK]) if slot == FAR else (k_in, v_in)
        return [
            remote(src.at[:, cols(c)], dst.at[slot, :, cols(c)], kv_ss.at[slot - 1, i, c], kv_rs.at[slot - 1, i, c], target)
            for i, (src, dst) in enumerate(zip(sources, (ks, vs)))
        ]

    def dq_copy(slot, c):
        target = to_near if slot == NEAR else to_across
        return remote(
            dq_send.at[slot - 1, :, cols(c)], dq_recv.at[slot - 1, :, cols(c)],
            dq_ss.at[slot - 1, c], dq_rs.at[slot - 1, c], target,
        )

    def dkv_copies(slot, target, c):
        return (
            remote(dk_send.at[slot - 1, :, cols(c)], dk_recv.at[slot - 1, :, cols(c)], dkv_ss.at[slot - 1, 0, c], dkv_rs.at[slot - 1, 0, c], target),
            remote(dv_send.at[slot - 1, :, cols(c)], dv_recv.at[slot - 1, :, cols(c)], dkv_ss.at[slot - 1, 1, c], dkv_rs.at[slot - 1, 1, c], target),
        )

    def is_via(c):
        return jnp.logical_and(c >= VIA_FIRST, c < VIA_LAST)

    def via_copies(c):
        return [
            remote(src.at[:, cols(c)], passing.at[i, :, cols(c - VIA_FIRST)], kv_ss.at[LINK - 1, i, c], pass_rs.at[i, c], to_near)
            for i, src in enumerate((k_in, v_in))
        ]

    def onward_copies(c):
        return [
            remote(passing.at[i, :, cols(c - VIA_FIRST)], dst.at[LINK, :, cols(c)], pass_ss.at[i, c], kv_rs.at[LINK - 1, i, c], to_cross)
            for i, dst in enumerate((ks, vs))
        ]

    def carry(c):
        for copy in via_copies(c):
            copy.wait_recv()
        for copy in onward_copies(c):
            copy.start()

    def loop(first, last, body):
        def run(c, carry):
            body(c)
            return carry

        lax.fori_loop(first, last, run, 0)

    def start_queries(c):
        @pl.when(jnp.logical_and(outer, is_via(c)))
        def _():
            for copy in via_copies(c):
                copy.start()
        for copy in query_copies(NEAR, c):
            copy.start()

        @pl.when(has_across)
        def _():
            for copy in query_copies(ACROSS, c):
                copy.start()

    def start_keys(c):
        for copy in key_copies(CHIP, to_chip, c):
            copy.start()

    def start_link_keys(c):
        for copy in key_copies(LINK, to_link, c):
            copy.start()

    loop(0, EARLY, start_queries)
    loop(0, chunks, start_keys)

    @pl.when(jnp.logical_and(inner, has_link))
    def _():
        loop(0, LEAD, start_link_keys)

    @pl.when(outer)
    def _():
        loop(0, VIA_FIRST, start_link_keys)
        loop(VIA_LAST, chunks, start_link_keys)

    for copy in local[:4]:
        copy.wait()
    aux[OWN] = jnp.zeros((AUX_ROWS, tile), F32)
    for h in range(heads):
        aux[OWN, h : h + 1, :] = lse_ref[h] * LOG2E
    ones = jnp.ones((8, width), LOW)

    def delta_row(h):
        products = gs[OWN, :, head_cols(h)].astype(F32) * outs[:, head_cols(h)].astype(F32)
        high = products.astype(LOW)
        low = (products - high.astype(F32)).astype(LOW)
        aux[OWN, pl.ds(DELTA_ROW + h, 1), :] = (dot(ones, high, NT) + dot(ones, low, NT))[0:1]

    loop(0, heads, delta_row)
    for i in range(9):
        if i == 4:
            line = jnp.zeros((1, tile), F32)
        else:
            line = jnp.where(jnp.full((1, tile), mask_ref[0, i], jnp.int32) > 0, 0.0, 1e30)
        aux[OWN, PEN_ROW + i : PEN_ROW + i + 1, :] = line
    aux_copy(NEAR).start()

    @pl.when(has_across)
    def _():
        aux_copy(ACROSS).start()

    loop(EARLY, chunks, start_queries)

    @pl.when(jnp.logical_not(has_across))
    def _():
        qs[ACROSS] = jnp.zeros((tile, full), LOW)
        gs[ACROSS] = jnp.zeros((tile, full), LOW)
        aux[ACROSS] = jnp.zeros((AUX_ROWS, tile), F32)

    for copy in local[4:]:
        copy.wait()
    aux_copy(NEAR).wait_recv()

    @pl.when(has_across)
    def _():
        aux_copy(ACROSS).wait_recv()

    for slot in (0, CHIP, LINK, FAR):
        for source, (query_frame, row_offset) in enumerate(query_frames):
            offset = jnp.clip(key_frames[slot] - query_frame, -1, 1)
            table = aux[source, PEN_ROW : PEN_ROW + 16, :]
            chosen = lax.broadcasted_iota(jnp.int32, table.shape, 0) == 3 * (offset + 1) + row_offset + 1
            line = jnp.sum(jnp.where(chosen, table, 0.0), 0, keepdims=True)
            pens[slot : slot + 1, source * tile : (source + 1) * tile] = line

    def pick(table, index):
        chosen = lax.broadcasted_iota(jnp.int32, table.shape, 0) == index
        return jnp.sum(jnp.where(chosen, table, 0.0), 0, keepdims=True)

    def pair_block(h, slot, sources):
        at = head_cols(h)
        first, count = sources[0], len(sources)
        span = slice(first * tile, (first + count) * tile)
        q = qs[first : first + count, :, at].reshape(count * tile, width)
        g = gs[first : first + count, :, at].reshape(count * tile, width)
        k, v = ks[slot, :, at], vs[slot, :, at]
        line = now[0:1, span] + pens[slot : slot + 1, span]
        weights = jnp.exp2(dot(k, q, NT) * (scale * LOG2E) - line)
        grad_score = (weights * (dot(v, g, NT) - now[1:2, span])).astype(LOW)
        dk = dot(grad_score, q, NN) * scale
        dv = dot(weights.astype(LOW), g, NN)
        return dk, dv, dot(k, grad_score, TN)

    ALL, PAIR, LAST = (OWN, NEAR, ACROSS), (OWN, NEAR), (ACROSS,)

    def finish_queries(h, source, total):
        part = total.T * scale
        if source == OWN:
            dq_own[:, head_cols(h)] = part
        else:
            dq_send[source - 1, :, head_cols(h)] = part.astype(LOW)

    def role(h, blocks, is_outer):
        at = head_cols(h)
        totals = {}
        for slot, sources in blocks:
            dk, dv, more = pair_block(h, slot, sources)
            for i, source in enumerate(sources):
                piece = more[:, i * tile : (i + 1) * tile]
                totals[source] = totals[source] + piece if source in totals else piece
            if slot == 0:
                dk_own[:, at], dv_own[:, at] = dk, dv
            elif slot == LINK and is_outer:
                held[lax.rem(h, 2), 0], held[lax.rem(h, 2), 1] = dk, dv
            else:
                dk_send[slot - 1, :, at] = dk.astype(LOW)
                dv_send[slot - 1, :, at] = dv.astype(LOW)
        for source, total in totals.items():
            if source == ACROSS and is_outer:
                across_sum[...] = total
            else:
                finish_queries(h, source, total)

    def send_link_grads(c):
        for copy in dkv_copies(LINK, to_link, c):
            copy.start()

    def merge(c):
        at = head_cols(c)
        for copy in dkv_copies(FAR, to_chip, c):
            copy.wait_recv()
        for i, (recv, send) in enumerate(((dk_recv, dk_send), (dv_recv, dv_send))):
            total = held[lax.rem(c, 2), i] + recv[FAR - 1, :, at].astype(F32)
            send[LINK - 1, :, at] = total.astype(LOW)
        send_link_grads(c)

    def compute(h):
        at = head_cols(h)
        for copy in query_copies(NEAR, h):
            copy.wait_recv()

        @pl.when(has_across)
        def _():
            for copy in query_copies(ACROSS, h):
                copy.wait_recv()

        @pl.when(jnp.logical_and(inner, is_via(h)))
        def _():
            carry(h)

        @pl.when(jnp.logical_and(jnp.logical_and(inner, has_link), h + LEAD < chunks))
        def _():
            start_link_keys(h + LEAD)

        for copy in key_copies(CHIP, to_chip, h):
            copy.wait_recv()

        @pl.when(has_link)
        def _():
            for copy in key_copies(LINK, to_link, h):
                copy.wait_recv()

        @pl.when(outer)
        def _():
            for copy in key_copies(FAR, to_chip, h):
                copy.start()

        for source in (OWN, NEAR, ACROSS):
            span = slice(source * tile, (source + 1) * tile)
            table = aux[source]
            now[0:1, span] = pick(table, h)
            now[1:2, span] = pick(table, DELTA_ROW + h)

        for here, blocks, is_outer in (
            (jnp.logical_and(outer, middle), ((0, ALL), (CHIP, PAIR), (LINK, ALL)), True),
            (jnp.logical_and(outer, jnp.logical_not(middle)), ((0, PAIR), (CHIP, PAIR), (LINK, LAST)), True),
            (jnp.logical_and(inner, middle), ((0, ALL), (CHIP, ALL), (LINK, ALL)), False),
            (jnp.logical_and(inner, jnp.logical_not(middle)), ((0, ALL), (CHIP, ALL)), False),
        ):
            @pl.when(here)
            def _():
                role(h, blocks, is_outer)

        for copy in dkv_copies(CHIP, to_chip, h):
            copy.start()
        dq_copy(NEAR, h).start()

        @pl.when(jnp.logical_and(inner, has_link))
        def _():
            send_link_grads(h)

        @pl.when(outer)
        def _():
            for copy in key_copies(FAR, to_chip, h):
                copy.wait_recv()
            dk, dv, more = pair_block(h, FAR, LAST)
            dk_send[FAR - 1, :, at] = dk.astype(LOW)
            dv_send[FAR - 1, :, at] = dv.astype(LOW)
            finish_queries(h, ACROSS, across_sum[...] + more)
            for copy in dkv_copies(FAR, to_chip, h):
                copy.start()

        @pl.when(has_across)
        def _():
            dq_copy(ACROSS, h).start()

        @pl.when(jnp.logical_and(outer, h >= 1))
        def _():
            merge(h - 1)

    loop(0, chunks, compute)

    @pl.when(outer)
    def _():
        merge(chunks - 1)

    @pl.when(jnp.logical_not(has_link))
    def _():
        dk_recv[LINK - 1] = jnp.zeros((tile, full), LOW)
        dv_recv[LINK - 1] = jnp.zeros((tile, full), LOW)

    @pl.when(jnp.logical_not(has_across))
    def _():
        dq_recv[ACROSS - 1] = jnp.zeros((tile, full), LOW)

    results = ((dq_own, dq_recv, qs.at[OWN]), (dk_own, dk_recv, ks.at[0]), (dv_own, dv_recv, vs.at[0]))

    def out_copy(i, c):
        out = (dq_out, dk_out, dv_out)[i]
        return pltpu.make_async_copy(results[i][2].at[:, cols(c)], out.at[:, cols(c)], out_sem.at[i, c])

    def last_pass(c):
        at = cols(c)
        dq_copy(NEAR, c).wait_recv()

        @pl.when(has_across)
        def _():
            dq_copy(ACROSS, c).wait_recv()

        for copy in dkv_copies(CHIP, to_chip, c):
            copy.wait_recv()
        @pl.when(has_link)
        def _():
            for copy in dkv_copies(LINK, to_link, c):
                copy.wait_recv()
        for i, (own, recv, stage) in enumerate(results):
            stage[:, at] = (own[:, at] + recv[0, :, at].astype(F32) + recv[1, :, at].astype(F32)).astype(LOW)
            out_copy(i, c).start()

    loop(0, chunks, last_pass)

    aux_copy(NEAR).wait_send()

    @pl.when(has_across)
    def _():
        aux_copy(ACROSS).wait_send()

    def drain(c):
        for i in range(3):
            out_copy(i, c).wait()
        for copy in (*query_copies(NEAR, c), dq_copy(NEAR, c)):
            copy.wait_send()

        @pl.when(has_across)
        def _():
            for copy in (*query_copies(ACROSS, c), dq_copy(ACROSS, c)):
                copy.wait_send()

        for copy in (*key_copies(CHIP, to_chip, c), *dkv_copies(CHIP, to_chip, c)):
            copy.wait_send()
        @pl.when(has_link)
        def _():
            for copy in (*key_copies(LINK, to_link, c), *dkv_copies(LINK, to_link, c)):
                copy.wait_send()
        @pl.when(outer)
        def _():
            for copy in (*key_copies(FAR, to_chip, c), *dkv_copies(FAR, to_chip, c)):
                copy.wait_send()

    loop(0, chunks, drain)

    def drain_carried(c):
        for copy in onward_copies(c):
            copy.wait_send()

    @pl.when(inner)
    def _():
        loop(VIA_FIRST, VIA_LAST, drain_carried)


def store_kernel(*refs):
    sources, targets, sem = refs[:3], refs[3:6], refs[6]
    copies = [pltpu.make_async_copy(a, b, sem.at[i]) for i, (a, b) in enumerate(zip(sources, targets))]
    for copy in copies:
        copy.start()
    for copy in copies:
        copy.wait()


def per_device(queries, keys, values, outputs, out_grads, log_sums, window_mask):
    shape = queries.shape
    tile, full = shape[2:]
    heads = log_sums.shape[2]
    width = full // heads
    chunks = heads
    flat = (tile, full)
    any_spec = pl.BlockSpec(memory_space=pl.ANY)
    vmem = pl.BlockSpec(memory_space=pltpu.VMEM)
    dma = pltpu.SemaphoreType.DMA
    grads = pl.pallas_call(
        kernel,
        out_shape=(jax.ShapeDtypeStruct(flat, LOW),) * 3,
        in_specs=[pl.BlockSpec(memory_space=pltpu.HBM)] * 7,
        out_specs=(any_spec,) * 3,
        scratch_shapes=[
            pltpu.VMEM((heads, 1, tile), F32),
            pltpu.SMEM((1, 9), jnp.int32),
            *[pltpu.VMEM((3,) + flat, LOW)] * 2,
            *[pltpu.VMEM((4,) + flat, LOW)] * 2,
            pltpu.VMEM((3, AUX_ROWS, tile), F32),
            pltpu.VMEM((8, 3 * tile), F32),
            pltpu.VMEM((8, 3 * tile), F32),
            pltpu.VMEM((width, tile), F32),
            pltpu.VMEM((2, 2, tile, width), F32),
            *[pltpu.VMEM(flat, F32)] * 3,
            pltpu.VMEM((2,) + flat, LOW), *[pltpu.VMEM((3,) + flat, LOW)] * 2,
            pltpu.VMEM((2,) + flat, LOW), *[pltpu.VMEM((3,) + flat, LOW)] * 2,
            pltpu.VMEM((2, tile, (VIA_LAST - VIA_FIRST) * width), LOW),
            dma((7,)), dma((3, chunks)), dma((2, chunks)), dma((2, chunks)),
            dma((2, 2, chunks)), dma((2, 2, chunks)),
            dma((3, 2, chunks)), dma((3, 2, chunks)),
            dma((2,)), dma((2,)),
            dma((2, chunks)), dma((2, chunks)),
            dma((3, 2, chunks)), dma((3, 2, chunks)),
        ],
        compiler_params=pltpu.CompilerParams(
            collective_id=0, has_side_effects=True, vmem_limit_bytes=50 * 2**20
        ),
        name="tile_attention_backward",
    )(
        *[x.reshape(flat) for x in (queries, keys, values, outputs, out_grads)],
        log_sums.reshape(heads, 1, tile),
        window_mask.reshape(1, -1),
    )
    stored = pl.pallas_call(
        store_kernel,
        out_shape=(jax.ShapeDtypeStruct(flat, LOW),) * 3,
        in_specs=[vmem] * 3,
        out_specs=(pl.BlockSpec(memory_space=pltpu.HBM),) * 3,
        scratch_shapes=[dma((3,))],
        compiler_params=pltpu.CompilerParams(vmem_limit_bytes=8 * 2**20),
        name="store_gradients",
    )(*grads)
    return tuple(g.reshape(shape) for g in stored)


def solution(mesh):
    tiles = P("tm", "space", None, None)
    return jax.shard_map(
        per_device,
        mesh=mesh,
        in_specs=(tiles,) * 6 + (P("tm", "space", None),),
        out_specs=(tiles,) * 3,
        check_vma=False,
    )
```
